512 devices in a mesh: frames: 128 (over z, x, core), heads: 4 (over y).
Axes of the slice: x: 4, y: 4, z: 16, core: 2. Of those that a mesh axis runs over, the one named last changes fastest.
Arguments:
- query_states: bfloat16 [256, 128, 1024], P('frames', 'heads'), may hold values from -6 to 6
- key_states: bfloat16 [256, 128, 1024], P('frames', 'heads'), may hold values from -6 to 6
- value_states: bfloat16 [256, 128, 1024], P('frames', 'heads'), may hold values from -6 to 6
- out_grad: bfloat16 [256, 128, 1024], P('frames', 'heads'), may hold values from -6 to 6
- partners: int32 [256, 6], replicated, may hold values from -1 to 255, as said below
Outputs:
- attended: bfloat16 [256, 128, 1024], P('frames', 'heads')
- query_grad: bfloat16 [256, 128, 1024], P('frames', 'heads')
- key_grad: bfloat16 [256, 128, 1024], P('frames', 'heads')
- value_grad: bfloat16 [256, 128, 1024], P('frames', 'heads')
The draws below stay inside these ranges and needn't reach their ends.
Inputs may be any that keep to these rules, and one draw needn't show every extreme that they name: `partners`: row f lists the frames that frame f attends to besides itself: distinct frames g other than f with |g - f| <= 6, followed by -1 in the unused slots. Every row lists at least one frame. In every draw some aligned group of 2 frames (k * 2 to k * 2 + 1) uses all 6 slots in each of its rows.
All inputs are finite; a program needn't handle non-finite values.
Results may differ from the reference program's by a relative error of at most 0.024.
Values may be sent and summed in bfloat16 or wider, within the bound.
A program may use at most 64 MiB of HBM per device.

```python
import jax
import jax.numpy as jnp
from jax import lax

HEADS = 16
HEAD_DIM = 64
FRAME_TOK = 128
FR_DEV = 2
SLOTS = 6
REACH = 3
WINDOW = 6
FRAMES = 256


def draw_query_states(key, part):
    base = jax.random.truncated_normal(jax.random.fold_in(key, 1), -4.0, 4.0, (FRAMES, FRAME_TOK, HEADS * HEAD_DIM), jnp.float32)
    return base.astype(jnp.bfloat16)


def draw_key_states(key, part):
    base = jax.random.truncated_normal(jax.random.fold_in(key, 2), -4.0, 4.0, (FRAMES, FRAME_TOK, HEADS * HEAD_DIM), jnp.float32)
    return base.astype(jnp.bfloat16)


def draw_partners(key, part):
    reach = REACH * FR_DEV
    offsets = jnp.concatenate([jnp.arange(-reach, 0), jnp.arange(1, reach + 1)]).astype(jnp.int32)
    row_keys = jax.random.split(jax.random.fold_in(key, 21), FRAMES)
    ranks = jax.vmap(lambda single: jax.random.permutation(single, 2 * reach))(row_keys).astype(jnp.int32)
    frame_ids = jnp.arange(FRAMES, dtype=jnp.int32)[:, None]
    candidate = frame_ids + offsets[None, :]
    inside = (candidate >= 0) & (candidate < FRAMES)
    order = jnp.argsort(jnp.where(inside, ranks, ranks + 2 * reach), axis=1)
    chosen = jnp.take_along_axis(candidate, order[:, :SLOTS], axis=1)
    groups = FRAMES // FR_DEV
    busy = jax.random.randint(jax.random.fold_in(key, 22), (groups,), 0, 4) == 0
    fullest = jax.random.randint(jax.random.fold_in(key, 23), (), 0, groups)
    busy = busy | (jnp.arange(groups) == fullest)
    busy_frames = jnp.repeat(busy, FR_DEV)
    many = jax.random.randint(jax.random.fold_in(key, 24), (FRAMES,), SLOTS - 1, SLOTS + 1)
    few = jax.random.randint(jax.random.fold_in(key, 25), (FRAMES,), 1, 3)
    degree = jnp.where(busy_frames, many, few)
    degree = jnp.where(jnp.arange(FRAMES) // FR_DEV == fullest, SLOTS, degree)
    slots = jnp.arange(SLOTS)[None, :]
    return jnp.where(slots < degree[:, None], chosen, -1).astype(jnp.int32)


def steps_of(rng, shape, shards, smallest, largest):
    gain, own = 1.0, jax.random.fold_in(rng, 6)
    for axis_at, parts in shards:
        heights = jnp.exp(jax.random.uniform(jax.random.fold_in(own, axis_at), (parts,), jnp.float32, smallest / len(shards), largest / len(shards)))
        gain = gain * jnp.repeat(heights, shape[axis_at] // parts).reshape([-1 if axis == axis_at else 1 for axis in range(len(shape))])
    return gain


def normal_values(stream_key, extent, scale, most, cuts=(), kind=jnp.bfloat16):
    entries = scale * jax.random.normal(stream_key, extent, jnp.float32)
    if cuts:
        entries = entries * steps_of(stream_key, extent, cuts, -0.22, 0.18)
    return jnp.clip(entries, -most, most).astype(kind)


def setup_inputs(seed: int = 0) -> dict:
    key_of = jax.random.split(jax.random.key(seed), 6)
    return {
        "query_states": draw_query_states(jax.random.fold_in(key_of[5], 71), 0),
        "key_states": draw_key_states(jax.random.fold_in(key_of[5], 71), 0),
        "value_states": normal_values(key_of[2], (FRAMES, FRAME_TOK, HEADS * HEAD_DIM), 1.0, 6.0, ((0, 128), (1, 4))),
        "out_grad": normal_values(key_of[3], (FRAMES, FRAME_TOK, HEADS * HEAD_DIM), 1.0, 6.0, ((0, 128), (1, 4))),
        "partners": draw_partners(jax.random.fold_in(key_of[5], 71), 0),
    }


def reference(query_states, key_states, value_states, out_grad, partners):
    scale = float(HEAD_DIM) ** -0.5
    highest = lax.Precision.HIGHEST
    frame_ids = jnp.arange(FRAMES, dtype=jnp.int32)

    def forward_frame(frame):
        keyset = jnp.concatenate([frame[None], partners[frame]]).astype(jnp.int32)
        present = keyset >= 0
        safe = jnp.where(present, keyset, 0).astype(jnp.int32)
        query = query_states[frame].astype(jnp.float32).reshape(FRAME_TOK, HEADS, HEAD_DIM)
        keyed = key_states[safe].astype(jnp.float32).reshape(SLOTS + 1, FRAME_TOK, HEADS, HEAD_DIM)
        valued = value_states[safe].astype(jnp.float32).reshape(SLOTS + 1, FRAME_TOK, HEADS, HEAD_DIM)
        scores = jnp.einsum("qhd,jkhd->hqjk", query, keyed, precision=highest) * scale
        scores = jnp.where(present[None, None, :, None], scores, -jnp.inf)
        peak = jnp.max(scores, axis=(2, 3))
        total = jnp.sum(jnp.exp(scores - peak[:, :, None, None]), axis=(2, 3))
        logsum = peak + jnp.log(total)
        weights = jnp.exp(scores - logsum[:, :, None, None])
        rounded = lax.optimization_barrier(weights.astype(jnp.bfloat16)).astype(jnp.float32)
        mixed = jnp.einsum("hqjk,jkhd->qhd", rounded, valued, precision=highest)
        attended = mixed.reshape(FRAME_TOK, HEADS * HEAD_DIM).astype(jnp.bfloat16)
        grad_out = out_grad[frame].astype(jnp.float32).reshape(FRAME_TOK, HEADS, HEAD_DIM)
        outcome = attended.astype(jnp.float32).reshape(FRAME_TOK, HEADS, HEAD_DIM)
        delta = jnp.sum(grad_out * outcome, axis=2).T
        prob_grad = jnp.einsum("qhd,jkhd->hqjk", grad_out, valued, precision=highest)
        score_grad = weights * (prob_grad - delta[:, :, None, None])
        score_grad = lax.optimization_barrier(score_grad.astype(jnp.bfloat16)).astype(jnp.float32)
        query_grad = jnp.einsum("hqjk,jkhd->qhd", score_grad, keyed, precision=highest) * scale
        query_grad = query_grad.reshape(FRAME_TOK, HEADS * HEAD_DIM).astype(jnp.bfloat16)
        return attended, query_grad, logsum, delta

    attended, query_grad, logsum, delta = lax.map(forward_frame, frame_ids)
    offsets = jnp.arange(-WINDOW, WINDOW + 1, dtype=jnp.int32)
    width = 2 * WINDOW + 1

    def key_frame(frame):
        sources = (frame + offsets).astype(jnp.int32)
        inside = (sources >= 0) & (sources < FRAMES)
        safe = jnp.where(inside, sources, 0).astype(jnp.int32)
        listed = jnp.any(partners[safe] == frame, axis=1)
        attends = inside & (listed | (sources == frame))
        queries = query_states[safe].astype(jnp.float32).reshape(width, FRAME_TOK, HEADS, HEAD_DIM)
        grads = out_grad[safe].astype(jnp.float32).reshape(width, FRAME_TOK, HEADS, HEAD_DIM)
        keyed = key_states[frame].astype(jnp.float32).reshape(FRAME_TOK, HEADS, HEAD_DIM)
        valued = value_states[frame].astype(jnp.float32).reshape(FRAME_TOK, HEADS, HEAD_DIM)
        scores = jnp.einsum("cqhd,khd->chqk", queries, keyed, precision=highest) * scale
        weights = jnp.exp(scores - logsum[safe][:, :, :, None])
        weights = jnp.where(attends[:, None, None, None], weights, 0.0)
        rounded = lax.optimization_barrier(weights.astype(jnp.bfloat16)).astype(jnp.float32)
        value_terms = jnp.einsum("chqk,cqhd->ckhd", rounded, grads, precision=highest)
        prob_grad = jnp.einsum("cqhd,khd->chqk", grads, valued, precision=highest)
        score_grad = weights * (prob_grad - delta[safe][:, :, :, None])
        score_grad = lax.optimization_barrier(score_grad.astype(jnp.bfloat16)).astype(jnp.float32)
        key_terms = jnp.einsum("chqk,cqhd->ckhd", score_grad, queries, precision=highest) * scale
        key_grad = jnp.sum(key_terms, axis=0).reshape(FRAME_TOK, HEADS * HEAD_DIM).astype(jnp.bfloat16)
        value_grad = jnp.sum(value_terms, axis=0).reshape(FRAME_TOK, HEADS * HEAD_DIM).astype(jnp.bfloat16)
        return key_grad, value_grad

    key_grad, value_grad = lax.map(key_frame, frame_ids)
    return attended, query_grad, key_grad, value_grad
```

```python
import functools

import jax
import jax.numpy as jnp
from jax import lax
from jax.experimental import pallas as pl
from jax.experimental.pallas import tpu as pltpu
from jax.sharding import PartitionSpec as P

HEAD_DIM = 64
SLOTS = 6
KEYS = SLOTS + 1
HALO = 6
OWN = 8
WIN = OWN + 2 * HALO
TOK = 128
HEADS = 16
ZERO = OWN * KEYS
MESH = pl.DeviceIdType.MESH
SCALE = float(HEAD_DIM) ** -0.5
OFFSETS = sorted(
    [(dx, dy) for dx in range(4) for dy in range(4)],
    key=lambda o: -(min(o[0], 4 - o[0]) + min(o[1], 4 - o[1])),
)


def kernel(
    chain,
    q_hbm,
    k_hbm,
    v_hbm,
    g_hbm,
    part_hbm,
    att_ref,
    qg_ref,
    kg_ref,
    vg_ref,
    inb,
    stage,
    win,
    wint,
    own_qd,
    sc,
    pd,
    terms,
    ret_out,
    ret_in,
    acc,
    outs,
    ostage,
    part,
    table,
    in_sem,
    part_sem,
    send_sem,
    recv_sem,
    halo_send,
    halo_recv,
    ret_send,
    ret_recv,
    out_send,
    out_recv,
):
    fi = lax.axis_index("frames")
    y = lax.axis_index("heads")
    z = lax.div(fi, 8)
    x = lax.rem(lax.div(fi, 2), 4)
    c = lax.rem(fi, 2)
    pos = z * 2 + c
    head = y * 4 + x
    up = jnp.where(c == 0, fi + 1, fi + 7)
    down = jnp.where(c == 1, fi - 1, fi - 7)
    has_up = pos < chain - 1
    has_down = pos > 0
    stays = lax.div(x, 2) == c

    loads = [
        pltpu.make_async_copy(ref, inb.at[i], in_sem.at[i])
        for i, ref in enumerate((k_hbm, v_hbm, q_hbm, g_hbm))
    ]
    for copy in loads:
        copy.start()
    part_copy = pltpu.make_async_copy(
        part_hbm.at[pl.ds(pl.multiple_of(pos * OWN, OWN), OWN), :], part, part_sem
    )
    part_copy.start()

    barrier = pltpu.get_barrier_semaphore()
    for j in range(2):
        for cs in range(2):
            for dy in range(4):
                ys = lax.rem(y + dy, 4)
                xs = 2 * c + j
                if dy == 0:

                    @pl.when(jnp.logical_or(xs != x, cs != c))
                    def _():
                        pl.semaphore_signal(
                            barrier, inc=1, device_id=(z * 8 + xs * 2 + cs, ys), device_id_type=MESH
                        )
                else:
                    pl.semaphore_signal(
                        barrier, inc=1, device_id=(z * 8 + xs * 2 + cs, ys), device_id_type=MESH
                    )

    @pl.when(has_up)
    def _():
        pl.semaphore_signal(barrier, inc=1, device_id=(up, y), device_id_type=MESH)

    @pl.when(has_down)
    def _():
        pl.semaphore_signal(barrier, inc=1, device_id=(down, y), device_id_type=MESH)

    lane = lax.broadcasted_iota(jnp.int32, (2, 32, 128), 2)
    low = lane < HEAD_DIM

    def turned(value):
        return jnp.concatenate([value[..., HEAD_DIM:], value[..., :HEAD_DIM]], axis=-1)

    def pack(kind, first, second, scale):
        for p in range(HEADS // 2):
            one = inb[first, :, :, p * 128 : (p + 1) * 128]
            two = inb[second, :, :, p * 128 : (p + 1) * 128]
            if scale:
                one = one * jnp.bfloat16(SCALE)
            stage[kind, 2 * p] = jnp.where(low, one, turned(two))
            stage[kind, 2 * p + 1] = jnp.where(low, turned(one), two)

    loads[0].wait()
    loads[1].wait()
    pack(0, 0, 1, False)
    loads[2].wait()
    loads[3].wait()
    pack(1, 2, 3, True)

    pl.semaphore_wait(
        barrier,
        16
        - stays.astype(jnp.int32)
        + has_up.astype(jnp.int32)
        + has_down.astype(jnp.int32),
    )

    pair = lax.rem(x, 2) * 2 + c
    rows = pl.ds(pl.multiple_of(y * 32, 32), 32)
    sends = []
    for kind in range(2):
        for i, (dx, dy) in enumerate(OFFSETS):
            xd = lax.rem(x + dx, 4)
            yd = lax.rem(y + dy, 4)
            src = stage.at[kind, yd * 4 + xd]
            if kind == 0:
                dst = win.at[pl.ds(HALO + 2 * pair, 2), rows, :]
            else:
                dst = own_qd.at[pl.ds(2 * pair, 2), rows, :]
            remote = pltpu.make_async_remote_copy(
                src_ref=src,
                dst_ref=dst,
                send_sem=send_sem.at[kind, i],
                recv_sem=recv_sem.at[kind, pair],
                device_id=(z * 8 + xd * 2 + lax.div(x, 2), yd),
                device_id_type=MESH,
            )
            if dx == 0 and dy == 0:
                local = pltpu.make_async_copy(src, dst, recv_sem.at[kind, pair])

                @pl.when(stays)
                def _():
                    local.start()

                @pl.when(jnp.logical_not(stays))
                def _():
                    remote.start()

                sends.append((True, remote))
            else:
                remote.start()
                sends.append((False, remote))

    part_copy.wait()

    base = pos * OWN - HALO

    @pl.loop(0, OWN)
    def _(f):
        for w in range(WIN):
            at = jnp.int32(ZERO)
            for s in range(SLOTS):
                at = jnp.where(part[f, s] - base == w, f * KEYS + 1 + s, at)
            at = jnp.where(f + HALO == w, f * KEYS, at)
            table[f, w] = at

    terms[ZERO] = jnp.zeros((TOK, 128), jnp.float32)

    @pl.when(jnp.logical_not(has_up))
    def _():
        win[HALO + OWN :] = jnp.zeros((HALO, TOK, 128), jnp.bfloat16)
        ret_in[0] = jnp.zeros((HALO, TOK, 128), jnp.bfloat16)

    @pl.when(jnp.logical_not(has_down))
    def _():
        win[:HALO] = jnp.zeros((HALO, TOK, 128), jnp.bfloat16)
        ret_in[1] = jnp.zeros((HALO, TOK, 128), jnp.bfloat16)

    halo_up = []
    halo_down = []
    for k in range(4):
        here = win.at[HALO + 2 * k : HALO + 2 * k + 2]
        pltpu.make_async_copy(here, here, recv_sem.at[0, k]).wait()
        if k >= 1:
            copy = pltpu.make_async_remote_copy(
                src_ref=here,
                dst_ref=win.at[2 * k - 2 : 2 * k],
                send_sem=halo_send.at[0, k - 1],
                recv_sem=halo_recv.at[0, k - 1],
                device_id=(up, y),
                device_id_type=MESH,
            )
            pl.when(has_up)(copy.start)
            halo_up.append(copy)
        if k <= 2:
            copy = pltpu.make_async_remote_copy(
                src_ref=here,
                dst_ref=win.at[HALO + OWN + 2 * k : HALO + OWN + 2 * k + 2],
                send_sem=halo_send.at[1, k],
                recv_sem=halo_recv.at[1, k],
                device_id=(down, y),
                device_id_type=MESH,
            )
            pl.when(has_down)(copy.start)
            halo_down.append(copy)

    def flip(w):
        wint[w] = win[w].T

    for f in range(OWN):
        flip(HALO + f)

    for copy in halo_up:
        pl.when(has_down)(copy.wait_recv)
    for copy in halo_down:
        pl.when(has_up)(copy.wait_recv)
    for w in range(HALO):
        flip(w)
        flip(HALO + OWN + w)
    for k in range(4):
        here = own_qd.at[2 * k : 2 * k + 2]
        pltpu.make_async_copy(here, here, recv_sem.at[1, k]).wait()

    half = lax.broadcasted_iota(jnp.int32, (TOK, 128), 1) < HEAD_DIM

    def one_frame(f):
        mixed = own_qd[f]
        none = jnp.zeros_like(mixed)
        qd = jnp.concatenate([jnp.where(half, none, mixed), jnp.where(half, mixed, none)], axis=0)
        at = [f + HALO]
        bias = [None]
        for s in range(SLOTS):
            partner = part[f, s]
            near = jnp.minimum(jnp.maximum(partner - base, 0), WIN - 1)
            at.append(jnp.where(partner >= 0, near, f + HALO))
            bias.append(jnp.where(partner >= 0, jnp.float32(0.0), jnp.float32(-jnp.inf)))
        peak = None
        for s in range(KEYS):
            both = lax.dot_general(
                win[at[s]], qd, (((1,), (1,)), ((), ())), preferred_element_type=jnp.float32
            )
            score = both[:, 128:]
            if bias[s] is not None:
                score = score + bias[s]
            sc[s, :, :128] = both[:, :128]
            sc[s, :, 128:] = score
            top = jnp.max(score.reshape(16, 8, 128), axis=0)
            peak = top if peak is None else jnp.maximum(peak, top)
        peak = jnp.max(peak, axis=0, keepdims=True)
        total = jnp.zeros((8, 128), jnp.float32)
        dsum = jnp.zeros((8, 128), jnp.float32)
        for s in range(KEYS):
            e = jnp.exp(sc[s, :, 128:] - peak)
            sc[s, :, 128:] = e
            total = total + jnp.sum(e.reshape(16, 8, 128), axis=0)
            dsum = dsum + jnp.sum((e * sc[s, :, :128]).reshape(16, 8, 128), axis=0)
        inv = 1.0 / jnp.sum(total, axis=0, keepdims=True)
        delta = jnp.sum(dsum, axis=0, keepdims=True) * inv
        for s in range(KEYS):
            w = sc[s, :, 128:] * inv
            pd[s * TOK : (s + 1) * TOK, :128] = w.astype(jnp.bfloat16)
            pd[s * TOK : (s + 1) * TOK, 128:] = (w * (sc[s, :, :128] - delta)).astype(jnp.bfloat16)
        prod = jnp.dot(pd[...], qd, preferred_element_type=jnp.float32)
        for s in range(KEYS):
            terms[f * KEYS + s] = prod[s * TOK : (s + 1) * TOK]
        turned_kv = jnp.concatenate([wint[at[s]] for s in range(KEYS)], axis=1)
        res = jnp.dot(turned_kv, pd[...], preferred_element_type=jnp.float32)
        outcome = jnp.concatenate([res[:HEAD_DIM, 128:] * SCALE, res[HEAD_DIM:, :128]], axis=0)
        outs[0, f] = outcome.T.astype(jnp.bfloat16)

    out_copies = []

    def give_back(kind, k):
        xs = 2 * c + k // 2
        cs = k % 2
        for dy in range(4):
            ys = lax.rem(y + dy, 4)
            src = outs.at[kind, 2 * k : 2 * k + 2, pl.ds(pl.multiple_of(ys * 32, 32), 32), :]
            dst = ostage.at[kind, head]
            remote = pltpu.make_async_remote_copy(
                src_ref=src,
                dst_ref=dst,
                send_sem=out_send.at[kind, k, dy],
                recv_sem=out_recv.at[kind],
                device_id=(z * 8 + xs * 2 + cs, ys),
                device_id_type=MESH,
            )
            if dy == 0:
                mine = jnp.logical_and(xs == x, cs == c)
                local = pltpu.make_async_copy(src, dst, out_recv.at[kind])
                pl.when(mine)(local.start)
                pl.when(jnp.logical_not(mine))(remote.start)
                out_copies.append((mine, remote))
            else:
                remote.start()
                out_copies.append((None, remote))

    @pl.loop(0, OWN)
    def _(f):
        one_frame(f)

    for k in range(4):
        give_back(0, k)

    def gathered(w):
        total = None
        for f in range(max(0, w - 2 * HALO), min(OWN, w + 1)):
            term = terms[table[f, w]]
            total = term if total is None else total + term
        return total

    for w in range(HALO):
        ret_out[0, w] = gathered(w).astype(jnp.bfloat16)
    back_down = pltpu.make_async_remote_copy(
        src_ref=ret_out.at[0],
        dst_ref=ret_in.at[0],
        send_sem=ret_send.at[0],
        recv_sem=ret_recv.at[0],
        device_id=(down, y),
        device_id_type=MESH,
    )
    pl.when(has_down)(back_down.start)
    for w in range(HALO):
        ret_out[1, w] = gathered(HALO + OWN + w).astype(jnp.bfloat16)
    back_up = pltpu.make_async_remote_copy(
        src_ref=ret_out.at[1],
        dst_ref=ret_in.at[1],
        send_sem=ret_send.at[1],
        recv_sem=ret_recv.at[1],
        device_id=(up, y),
        device_id_type=MESH,
    )
    pl.when(has_up)(back_up.start)
    for f in range(OWN):
        acc[f] = gathered(HALO + f)
    pl.when(has_up)(back_down.wait_recv)
    pl.when(has_down)(back_up.wait_recv)
    for k in range(4):
        for f in (2 * k, 2 * k + 1):
            total = acc[f]
            if f >= 2:
                total = total + ret_in[0, f - 2].astype(jnp.float32)
            if f < HALO:
                total = total + ret_in[1, f].astype(jnp.float32)
            outs[1, f] = total.astype(jnp.bfloat16)
        give_back(1, k)

    def unpack(kind, one_ref, two_ref):
        pltpu.make_async_copy(ostage.at[kind], ostage.at[kind], out_recv.at[kind]).wait()
        for p in range(HEADS // 2):
            even = ostage[kind, 2 * p]
            odd = ostage[kind, 2 * p + 1]
            one_ref[:, :, p * 128 : (p + 1) * 128] = jnp.where(low, even, turned(odd))
            two_ref[:, :, p * 128 : (p + 1) * 128] = jnp.where(low, turned(even), odd)

    unpack(0, qg_ref, att_ref)
    unpack(1, kg_ref, vg_ref)

    for local_too, remote in sends:
        if local_too:
            pl.when(jnp.logical_not(stays))(remote.wait_send)
        else:
            remote.wait_send()
    for copy in halo_up:
        pl.when(has_up)(copy.wait_send)
    for copy in halo_down:
        pl.when(has_down)(copy.wait_send)
    pl.when(has_down)(back_down.wait_send)
    pl.when(has_up)(back_up.wait_send)
    for mine, remote in out_copies:
        if mine is None:
            remote.wait_send()
        else:
            pl.when(jnp.logical_not(mine))(remote.wait_send)


def per_device(query, keyed, valued, grad_out, partners):
    chain = lax.axis_size("frames") // 4
    shape = jax.ShapeDtypeStruct(query.shape, jnp.bfloat16)
    dma = pltpu.SemaphoreType.DMA
    return pl.pallas_call(
        functools.partial(kernel, chain),
        out_shape=(shape,) * 4,
        in_specs=[pl.BlockSpec(memory_space=pl.ANY)] * 5,
        out_specs=(pl.BlockSpec(memory_space=pltpu.VMEM),) * 4,
        scratch_shapes=[
            pltpu.VMEM((4, 2, 32, 1024), jnp.bfloat16),
            pltpu.VMEM((2, HEADS, 2, 32, 128), jnp.bfloat16),
            pltpu.VMEM((WIN, TOK, 128), jnp.bfloat16),
            pltpu.VMEM((WIN, 128, TOK), jnp.bfloat16),
            pltpu.VMEM((OWN, TOK, 128), jnp.bfloat16),
            pltpu.VMEM((KEYS, TOK, 256), jnp.float32),
            pltpu.VMEM((KEYS * TOK, 256), jnp.bfloat16),
            pltpu.VMEM((ZERO + 1, TOK, 128), jnp.float32),
            pltpu.VMEM((2, HALO, TOK, 128), jnp.bfloat16),
            pltpu.VMEM((2, HALO, TOK, 128), jnp.bfloat16),
            pltpu.VMEM((OWN, TOK, 128), jnp.float32),
            pltpu.VMEM((2, OWN, TOK, 128), jnp.bfloat16),
            pltpu.VMEM((2, HEADS, 2, 32, 128), jnp.bfloat16),
            pltpu.SMEM((OWN, SLOTS), jnp.int32),
            pltpu.SMEM((OWN, WIN), jnp.int32),
            dma((4,)),
            dma(()),
            dma((2, 16)),
            dma((2, 4)),
            dma((2, 3)),
            dma((2, 3)),
            dma((2,)),
            dma((2,)),
            dma((2, 4, 4)),
            dma((2,)),
        ],
        compiler_params=pltpu.CompilerParams(
            collective_id=0, has_side_effects=True, vmem_limit_bytes=48 * 2**20
        ),
    )(query, keyed, valued, grad_out, partners)


def solution(mesh):
    spec = P("frames", "heads", None)
    return jax.shard_map(
        per_device,
        mesh=mesh,
        in_specs=(spec, spec, spec, spec, P()),
        out_specs=(spec,) * 4,
        check_vma=False,
    )
```

```python
import functools

import jax
import jax.numpy as jnp
from jax import lax
from jax.experimental import pallas as pl
from jax.experimental.pallas import tpu as pltpu
from jax.sharding import PartitionSpec as P

HEAD_DIM = 64
SLOTS = 6
KEYS = SLOTS + 1
HALO = 6
OWN = 8
WIN = OWN + 2 * HALO
TOK = 128
HEADS = 16
ZERO = OWN * KEYS
MESH = pl.DeviceIdType.MESH
SCALE = float(HEAD_DIM) ** -0.5
OFFSETS = sorted(
    [(dx, dy) for dx in range(4) for dy in range(4)],
    key=lambda o: -(min(o[0], 4 - o[0]) + min(o[1], 4 - o[1])),
)


def turned(value):
    return jnp.concatenate([value[..., HEAD_DIM:], value[..., :HEAD_DIM]], axis=-1)


def unpack_kernel(staged, att_hbm, qg_hbm, kg_hbm, vg_hbm, taken, whole, in_sem, sem):
    low = lax.broadcasted_iota(jnp.int32, (2, 32, 128), 2) < HEAD_DIM
    outs = (qg_hbm, att_hbm, kg_hbm, vg_hbm)
    loads = {}
    for kind in (0, 2, 1):
        for h in range(2):
            at = (kind, slice(h * 8, (h + 1) * 8))
            loads[kind, h] = pltpu.make_async_copy(staged.at[at], taken.at[at], in_sem.at[kind, h])
            loads[kind, h].start()
    copies = []
    for kind in range(2):
        for p in range(HEADS // 2):
            if p % 4 == 0:
                loads[kind, p // 4].wait()
                if kind == 1:
                    loads[2, p // 4].wait()
            at = slice(p * 128, (p + 1) * 128)
            even = taken[kind, 2 * p]
            odd = taken[kind, 2 * p + 1]
            if kind == 1:
                even = even + taken[2, 2 * p]
                odd = odd + taken[2, 2 * p + 1]
            whole[2 * kind, :, :, at] = jnp.where(low, even, turned(odd))
            whole[2 * kind + 1, :, :, at] = jnp.where(low, turned(even), odd)
        for i in (2 * kind, 2 * kind + 1):
            copies.append(pltpu.make_async_copy(whole.at[i], outs[i], sem.at[i]))
            copies[-1].start()
    for copy in copies:
        copy.wait()


def unpacked(staged, shape):
    return pl.pallas_call(
        unpack_kernel,
        out_shape=(jax.ShapeDtypeStruct(shape, jnp.bfloat16),) * 4,
        in_specs=[pl.BlockSpec(memory_space=pltpu.HBM)],
        out_specs=(pl.BlockSpec(memory_space=pltpu.HBM),) * 4,
        scratch_shapes=[
            pltpu.VMEM(staged.shape, jnp.bfloat16),
            pltpu.VMEM((4,) + shape, jnp.bfloat16),
            pltpu.SemaphoreType.DMA((3, 2)),
            pltpu.SemaphoreType.DMA((4,)),
        ],
    )(staged)


def kernel(
    depth,
    q_hbm,
    k_hbm,
    v_hbm,
    g_hbm,
    part_hbm,
    ostage,
    inb,
    stage,
    win,
    wint,
    own_qd,
    sc,
    pd,
    terms,
    cross_out,
    die_out,
    die_in,
    outs,
    blank,
    part,
    table,
    in_sem,
    part_sem,
    send_sem,
    recv_sem,
    cross_send,
    cross_recv,
    die_send,
    die_recv,
    ret_send,
    ret_recv,
    out_send,
    cross_out_send,
    out_recv,
):
    fi = lax.axis_index("frames")
    y = lax.axis_index("heads")
    z = lax.div(fi, 8)
    x = lax.rem(lax.div(fi, 2), 4)
    c = lax.rem(fi, 2)
    pos = z * 2 + c
    head = y * 4 + x
    home = lax.div(x, 2)
    pair = lax.rem(x, 2) * 2 + c
    stays = home == c
    partner = fi + 1 - 2 * c
    ahead = jnp.logical_and(jnp.logical_and(home == 1, pair >= 1), z < depth - 1)
    behind = jnp.logical_and(jnp.logical_and(home == 0, pair <= 2), z > 0)
    crosses = jnp.logical_or(ahead, behind)
    has_cross = jnp.logical_or(jnp.logical_and(c == 1, z < depth - 1), jnp.logical_and(c == 0, z > 0))

    loads = [
        pltpu.make_async_copy(ref, inb.at[i], in_sem.at[i])
        for i, ref in enumerate((k_hbm, v_hbm, q_hbm, g_hbm))
    ]
    for copy in loads:
        copy.start()
    part_copy = pltpu.make_async_copy(part_hbm, part, part_sem)
    part_copy.start()

    barrier = pltpu.get_barrier_semaphore()

    def greet(frame_at, head_at):
        pl.semaphore_signal(barrier, inc=1, device_id=(frame_at, head_at), device_id_type=MESH)

    other = z + 2 * c - 1
    for j in range(2):
        for cs in range(2):
            xs = 2 * c + j
            xo = 2 * (1 - c) + j
            for dy in range(4):
                ys = lax.rem(y + dy, 4)
                if dy == 0:

                    @pl.when(jnp.logical_or(xs != x, cs != c))
                    def _():
                        greet(z * 8 + xs * 2 + cs, ys)
                else:
                    greet(z * 8 + xs * 2 + cs, ys)
            if (j, cs) == (0, 0):
                wanted = jnp.logical_and(has_cross, c == 1)
            elif (j, cs) == (1, 1):
                wanted = jnp.logical_and(has_cross, c == 0)
            else:
                wanted = has_cross

            @pl.when(wanted)
            def _():
                for dy in range(4):
                    greet(other * 8 + xo * 2 + cs, lax.rem(y + dy, 4))

    greet(partner, y)

    low = lax.broadcasted_iota(jnp.int32, (2, 32, 128), 2) < HEAD_DIM

    def pack(kind, first, second, scale):
        for p in range(HEADS // 2):
            one = inb[first, :, :, p * 128 : (p + 1) * 128]
            two = inb[second, :, :, p * 128 : (p + 1) * 128]
            if scale:
                one = one * jnp.bfloat16(SCALE)
            stage[kind, 2 * p] = jnp.where(low, one, turned(two))
            stage[kind, 2 * p + 1] = jnp.where(low, turned(one), two)

    loads[0].wait()
    loads[1].wait()
    pack(0, 0, 1, False)
    loads[2].wait()
    loads[3].wait()
    pack(1, 2, 3, True)

    pl.semaphore_wait(
        barrier, 17 - stays.astype(jnp.int32) + 16 * crosses.astype(jnp.int32)
    )

    rows = pl.ds(pl.multiple_of(y * 32, 32), 32)

    def to_slab(kind, i, act):
        dx, dy = OFFSETS[i]
        xd = lax.rem(x + dx, 4)
        yd = lax.rem(y + dy, 4)
        src = stage.at[kind, yd * 4 + xd]
        if kind == 0:
            dst = win.at[pl.ds(HALO + 2 * pair, 2), rows, :]
        else:
            dst = own_qd.at[pl.ds(2 * pair, 2), rows, :]
        remote = pltpu.make_async_remote_copy(
            src_ref=src,
            dst_ref=dst,
            send_sem=send_sem.at[kind, i],
            recv_sem=recv_sem.at[kind, pair],
            device_id=(z * 8 + xd * 2 + home, yd),
            device_id_type=MESH,
        )
        if dx == 0 and dy == 0:
            if act == "start":
                local = pltpu.make_async_copy(src, dst, recv_sem.at[kind, pair])
                pl.when(stays)(local.start)
                pl.when(jnp.logical_not(stays))(remote.start)
            else:
                pl.when(jnp.logical_not(stays))(remote.wait_send)
        elif act == "start":
            remote.start()
        else:
            remote.wait_send()

    def to_next_slab(i, act):
        dx, dy = OFFSETS[i]
        xd = lax.rem(x + dx, 4)
        yd = lax.rem(y + dy, 4)
        land = jnp.where(home == 1, 2 * pair - 2, HALO + OWN + 2 * pair)
        remote = pltpu.make_async_remote_copy(
            src_ref=stage.at[0, yd * 4 + xd],
            dst_ref=win.at[pl.ds(land, 2), rows, :],
            send_sem=cross_send.at[i],
            recv_sem=cross_recv,
            device_id=((z + 2 * home - 1) * 8 + xd * 2 + 1 - home, yd),
            device_id_type=MESH,
        )
        if act == "start":
            remote.start()
        else:
            remote.wait_send()

    for i in range(16):
        to_slab(0, i, "start")

    @pl.when(crosses)
    def _():
        for i in range(16):
            to_next_slab(i, "start")

    for i in range(16):
        to_slab(1, i, "start")

    part_copy.wait()

    base = pos * OWN - HALO

    def turned_frame(i):
        return jnp.where(c == 0, i, OWN - 1 - i)

    @pl.loop(0, OWN)
    def _(i):
        f = turned_frame(i)
        at_frame = pos * OWN + f
        for w in range(WIN):
            target = base + jnp.where(c == 0, w, WIN - 1 - w)
            at = jnp.int32(ZERO)
            for s in range(SLOTS):
                at = jnp.where(part[s, at_frame] == target, i * KEYS + 1 + s, at)
            table[i, w] = jnp.where(i + HALO == w, i * KEYS, at)

    terms[ZERO] = jnp.zeros((TOK, 128), jnp.float32)
    near = jnp.where(c == 0, HALO + OWN, 0)
    far = jnp.where(c == 0, 0, HALO + OWN)

    blank_copy = pltpu.make_async_copy(blank, ostage.at[2], out_recv.at[2])

    @pl.when(jnp.logical_not(crosses))
    def _():
        blank[...] = jnp.zeros_like(blank)
        blank_copy.start()

    @pl.when(jnp.logical_not(has_cross))
    def _():
        win[pl.ds(far, HALO)] = jnp.zeros((HALO, TOK, 128), jnp.bfloat16)

    def own_pair(k):
        return win.at[pl.ds(HALO + 2 * k, 2)]

    def byte_wait(ref, sem):
        pltpu.make_async_copy(ref, ref, sem).wait()

    def flip(w):
        wint[w] = win[w].T

    die_copies = []
    for j in range(3):
        k = j + 1 - c
        byte_wait(own_pair(k), recv_sem.at[0, k])
        copy = pltpu.make_async_remote_copy(
            src_ref=own_pair(k),
            dst_ref=win.at[pl.ds((HALO + OWN) * c + 2 * j, 2)],
            send_sem=die_send.at[j],
            recv_sem=die_recv.at[j],
            device_id=(partner, y),
            device_id_type=MESH,
        )
        copy.start()
        die_copies.append(copy)
    byte_wait(own_pair(3 * c), recv_sem.at[0, 3 * c])
    for f in range(OWN):
        flip(HALO + f)
    for copy in die_copies:
        copy.wait_recv()
    for w in range(HALO):
        flip(near + w)

    @pl.when(has_cross)
    def _():
        byte_wait(win.at[pl.ds(far, HALO)], cross_recv)

    for w in range(HALO):
        flip(far + w)
    for k in range(4):
        byte_wait(own_qd.at[2 * k : 2 * k + 2], recv_sem.at[1, k])

    half = lax.broadcasted_iota(jnp.int32, (TOK, 128), 1) < HEAD_DIM

    def one_frame(i):
        u = i % 2
        f = turned_frame(i)
        mixed = own_qd[f]
        none = jnp.zeros_like(mixed)
        qd = jnp.concatenate([jnp.where(half, none, mixed), jnp.where(half, mixed, none)], axis=0)
        at = [f + HALO]
        bias = [None]
        for s in range(SLOTS):
            listed = part[s, pos * OWN + f]
            close = jnp.minimum(jnp.maximum(listed - base, 0), WIN - 1)
            at.append(jnp.where(listed >= 0, close, f + HALO))
            bias.append(jnp.where(listed >= 0, jnp.float32(0.0), jnp.float32(-jnp.inf)))
        peak = None
        for s in range(KEYS):
            both = lax.dot_general(
                win[at[s]], qd, (((1,), (1,)), ((), ())), preferred_element_type=jnp.float32
            )
            score = both[:, 128:]
            if bias[s] is not None:
                score = score + bias[s]
            sc[u, s, :, :128] = both[:, :128]
            sc[u, s, :, 128:] = score
            top = jnp.max(score.reshape(16, 8, 128), axis=0)
            peak = top if peak is None else jnp.maximum(peak, top)
        peak = jnp.max(peak, axis=0, keepdims=True)
        total = jnp.zeros((8, 128), jnp.float32)
        dsum = jnp.zeros((8, 128), jnp.float32)
        for s in range(KEYS):
            e = jnp.exp(sc[u, s, :, 128:] - peak)
            sc[u, s, :, 128:] = e
            total = total + jnp.sum(e.reshape(16, 8, 128), axis=0)
            dsum = dsum + jnp.sum((e * sc[u, s, :, :128]).reshape(16, 8, 128), axis=0)
        inv = 1.0 / jnp.sum(total, axis=0, keepdims=True)
        delta = jnp.sum(dsum, axis=0, keepdims=True) * inv
        for s in range(KEYS):
            w = sc[u, s, :, 128:] * inv
            rows_at = slice(s * TOK, (s + 1) * TOK)
            pd[u, rows_at, :128] = w.astype(jnp.bfloat16)
            pd[u, rows_at, 128:] = (w * (sc[u, s, :, :128] - delta)).astype(jnp.bfloat16)
        prod = jnp.dot(pd[u], qd, preferred_element_type=jnp.float32)
        for s in range(KEYS):
            terms[i * KEYS + s] = prod[s * TOK : (s + 1) * TOK]
        turned_kv = jnp.concatenate([wint[at[s]] for s in range(KEYS)], axis=1)
        res = jnp.dot(turned_kv, pd[u], preferred_element_type=jnp.float32)
        outcome = jnp.concatenate([res[:HEAD_DIM, 128:] * SCALE, res[HEAD_DIM:, :128]], axis=0)
        outs[0, f] = outcome.T.astype(jnp.bfloat16)

    def gathered(w):
        total = None
        for i in range(max(0, w - 2 * HALO), min(OWN, w + 1)):
            term = terms[table[i, w]]
            total = term if total is None else total + term
        return total

    def pair_of(j):
        return jnp.where(c == 0, j, 3 - j)

    def give_back(kind, j, act):
        k = pair_of(j)
        xs = 2 * c + lax.div(k, 2)
        cs = lax.rem(k, 2)
        for dy in range(4):
            ys = lax.rem(y + (2, 1, 3, 0)[dy], 4)
            src = outs.at[kind, pl.ds(2 * k, 2), pl.ds(pl.multiple_of(ys * 32, 32), 32), :]
            dst = ostage.at[kind, head]
            remote = pltpu.make_async_remote_copy(
                src_ref=src,
                dst_ref=dst,
                send_sem=out_send.at[kind, j, dy],
                recv_sem=out_recv.at[kind],
                device_id=(z * 8 + xs * 2 + cs, ys),
                device_id_type=MESH,
            )
            if dy == 3:
                mine = jnp.logical_and(xs == x, cs == c)
                if act == "start":
                    local = pltpu.make_async_copy(src, dst, out_recv.at[kind])
                    pl.when(mine)(local.start)
                    pl.when(jnp.logical_not(mine))(remote.start)
                else:
                    pl.when(jnp.logical_not(mine))(remote.wait_send)
            elif act == "start":
                remote.start()
            else:
                remote.wait_send()

    def give_across(j, act):
        k = jnp.where(c == 0, 1 + j, 2 - j)
        xs = 2 * (1 - c) + lax.div(k, 2)
        cs = lax.rem(k, 2)
        for dy in range(4):
            ys = lax.rem(y + (2, 1, 3, 0)[dy], 4)
            remote = pltpu.make_async_remote_copy(
                src_ref=cross_out.at[j, :, pl.ds(pl.multiple_of(ys * 32, 32), 32), :],
                dst_ref=ostage.at[2, head],
                send_sem=cross_out_send.at[j, dy],
                recv_sem=out_recv.at[2],
                device_id=(other * 8 + xs * 2 + cs, ys),
                device_id_type=MESH,
            )
            if act == "start":
                remote.start()
            else:
                remote.wait_send()

    for j in range(4):
        one_frame(2 * j)
        one_frame(2 * j + 1)
        give_back(0, j, "start")
        if j < 3:

            @pl.when(has_cross)
            def _():
                for half_at in range(2):
                    place = jnp.where(c == 0, half_at, 1 - half_at)
                    cross_out[j, place] = gathered(2 * j + half_at).astype(jnp.bfloat16)
                give_across(j, "start")

    ret_copies = []
    for j in range(3):
        for q in (2 * j, 2 * j + 1):
            die_out[q] = gathered(HALO + OWN + q).astype(jnp.bfloat16)
        copy = pltpu.make_async_remote_copy(
            src_ref=die_out.at[2 * j : 2 * j + 2],
            dst_ref=die_in.at[2 * j : 2 * j + 2],
            send_sem=ret_send.at[j],
            recv_sem=ret_recv.at[j],
            device_id=(partner, y),
            device_id_type=MESH,
        )
        copy.start()
        ret_copies.append(copy)
    for j in (0, 3, 2, 1):
        sums = [gathered(HALO + i) for i in (2 * j, 2 * j + 1)]
        if j > 0:
            ret_copies[3 - j].wait_recv()
        for n, i in enumerate((2 * j, 2 * j + 1)):
            total = sums[n]
            if j > 0:
                total = total + die_in[OWN - 1 - i].astype(jnp.float32)
            outs[1, turned_frame(i)] = total.astype(jnp.bfloat16)
        give_back(1, j, "start")

    for i in range(16):
        to_slab(0, i, "wait")
        to_slab(1, i, "wait")

    @pl.when(crosses)
    def _():
        for i in range(16):
            to_next_slab(i, "wait")

    for copy in die_copies + ret_copies:
        copy.wait_send()
    for j in range(4):
        give_back(0, j, "wait")
        give_back(1, j, "wait")

    @pl.when(has_cross)
    def _():
        for j in range(3):
            give_across(j, "wait")

    for kind in range(3):
        byte_wait(ostage.at[kind], out_recv.at[kind])


def per_device(query, keyed, valued, grad_out, partners):
    depth = lax.axis_size("frames") // 8
    dma = pltpu.SemaphoreType.DMA
    staged = pl.pallas_call(
        functools.partial(kernel, depth),
        out_shape=jax.ShapeDtypeStruct((3, HEADS, 2, 32, 128), jnp.bfloat16),
        in_specs=[pl.BlockSpec(memory_space=pltpu.HBM)] * 5,
        out_specs=pl.BlockSpec(memory_space=pltpu.HBM),
        scratch_shapes=[
            pltpu.VMEM((4, 2, 32, 1024), jnp.bfloat16),
            pltpu.VMEM((2, HEADS, 2, 32, 128), jnp.bfloat16),
            pltpu.VMEM((WIN, TOK, 128), jnp.bfloat16),
            pltpu.VMEM((WIN, 128, TOK), jnp.bfloat16),
            pltpu.VMEM((OWN, TOK, 128), jnp.bfloat16),
            pltpu.VMEM((2, KEYS, TOK, 256), jnp.float32),
            pltpu.VMEM((2, KEYS * TOK, 256), jnp.bfloat16),
            pltpu.VMEM((ZERO + 1, TOK, 128), jnp.float32),
            pltpu.VMEM((3, 2, TOK, 128), jnp.bfloat16),
            pltpu.VMEM((HALO, TOK, 128), jnp.bfloat16),
            pltpu.VMEM((HALO, TOK, 128), jnp.bfloat16),
            pltpu.VMEM((2, OWN, TOK, 128), jnp.bfloat16),
            pltpu.VMEM((HEADS, 2, 32, 128), jnp.bfloat16),
            pltpu.SMEM(partners.shape[::-1], jnp.int32),
            pltpu.SMEM((OWN, WIN), jnp.int32),
            dma((4,)),
            dma(()),
            dma((2, 16)),
            dma((2, 4)),
            dma((16,)),
            dma(()),
            dma((3,)),
            dma((3,)),
            dma((3,)),
            dma((3,)),
            dma((2, 4, 4)),
            dma((3, 4)),
            dma((3,)),
        ],
        compiler_params=pltpu.CompilerParams(collective_id=0, has_side_effects=True),
    )(query, keyed, valued, grad_out, partners.T)
    return unpacked(staged, query.shape)


def solution(mesh):
    spec = P("frames", "heads", None)
    return jax.shard_map(
        per_device,
        mesh=mesh,
        in_specs=(spec, spec, spec, spec, P()),
        out_specs=(spec,) * 4,
        check_vma=False,
    )
```

```python
import functools

import jax
import jax.numpy as jnp
from jax import lax
from jax.experimental import pallas as pl
from jax.experimental.pallas import tpu as pltpu
from jax.sharding import PartitionSpec as P

HEAD_DIM = 64
SLOTS = 6
KEYS = SLOTS + 1
HALO = 6
OWN = 8
WIN = OWN + 2 * HALO
TOK = 128
HEADS = 16
ZERO = OWN * KEYS
MESH = pl.DeviceIdType.MESH
SCALE = float(HEAD_DIM) ** -0.5
OFFSETS = sorted(
    [(dx, dy) for dx in range(4) for dy in range(4)],
    key=lambda o: -(min(o[0], 4 - o[0]) + min(o[1], 4 - o[1])),
)


def turned(value):
    return jnp.concatenate([value[..., HEAD_DIM:], value[..., :HEAD_DIM]], axis=-1)


def unpack_kernel(staged, att_hbm, qg_hbm, kg_hbm, vg_hbm, taken, whole, in_sem, sem):
    low = lax.broadcasted_iota(jnp.int32, (2, 32, 128), 2) < HEAD_DIM
    outs = (qg_hbm, att_hbm, kg_hbm, vg_hbm)
    loads = []
    for kind in range(2):
        for h in range(2):
            at = (kind, slice(h * 8, (h + 1) * 8))
            loads.append(pltpu.make_async_copy(staged.at[at], taken.at[at], in_sem.at[kind, h]))
            loads[-1].start()
    copies = []
    for kind in range(2):
        for p in range(HEADS // 2):
            if p % 4 == 0:
                loads[2 * kind + p // 4].wait()
            at = slice(p * 128, (p + 1) * 128)
            even = taken[kind, 2 * p]
            odd = taken[kind, 2 * p + 1]
            whole[2 * kind, :, :, at] = jnp.where(low, even, turned(odd))
            whole[2 * kind + 1, :, :, at] = jnp.where(low, turned(even), odd)
        for i in (2 * kind, 2 * kind + 1):
            copies.append(pltpu.make_async_copy(whole.at[i], outs[i], sem.at[i]))
            copies[-1].start()
    for copy in copies:
        copy.wait()


def unpacked(staged, shape):
    return pl.pallas_call(
        unpack_kernel,
        out_shape=(jax.ShapeDtypeStruct(shape, jnp.bfloat16),) * 4,
        in_specs=[pl.BlockSpec(memory_space=pltpu.HBM)],
        out_specs=(pl.BlockSpec(memory_space=pltpu.HBM),) * 4,
        scratch_shapes=[
            pltpu.VMEM(staged.shape, jnp.bfloat16),
            pltpu.VMEM((4,) + shape, jnp.bfloat16),
            pltpu.SemaphoreType.DMA((2, 2)),
            pltpu.SemaphoreType.DMA((4,)),
        ],
    )(staged)


def kernel(
    depth,
    q_hbm,
    k_hbm,
    v_hbm,
    g_hbm,
    part_hbm,
    ostage,
    inb,
    stage,
    win,
    wint,
    own_qd,
    sc,
    pd,
    terms,
    peaks,
    cross_out,
    cross_in,
    die_out,
    die_in,
    outs,
    part,
    table,
    in_sem,
    part_sem,
    send_sem,
    kv_recv,
    qd_recv,
    halo_send,
    halo_recv,
    cross_send,
    cross_recv,
    ret_send,
    ret_recv,
    out_send,
    out_recv,
):
    fi = lax.axis_index("frames")
    y = lax.axis_index("heads")
    z = lax.div(fi, 8)
    x = lax.rem(lax.div(fi, 2), 4)
    c = lax.rem(fi, 2)
    pos = z * 2 + c
    head = y * 4 + x
    home = lax.div(x, 2)
    pair = lax.rem(x, 2) * 2 + c
    stays = home == c
    partner = fi + 1 - 2 * c
    up = jnp.where(c == 0, fi + 1, fi + 7)
    down = jnp.where(c == 1, fi - 1, fi - 7)
    has_up = pos < 2 * depth - 1
    has_down = pos > 0
    has_cross = jnp.logical_or(jnp.logical_and(c == 1, has_up), jnp.logical_and(c == 0, has_down))
    across = jnp.where(c == 0, down, up)

    loads = [
        pltpu.make_async_copy(ref, inb.at[i], in_sem.at[i])
        for i, ref in enumerate((k_hbm, v_hbm, q_hbm, g_hbm))
    ]
    for copy in loads:
        copy.start()
    part_copy = pltpu.make_async_copy(part_hbm, part, part_sem)
    part_copy.start()

    barrier = pltpu.get_barrier_semaphore()

    def greet(frame_at, head_at):
        pl.semaphore_signal(barrier, inc=1, device_id=(frame_at, head_at), device_id_type=MESH)

    for j in range(2):
        for cs in range(2):
            xs = 2 * c + j
            for dy in range(4):
                ys = lax.rem(y + dy, 4)
                if dy == 0:

                    @pl.when(jnp.logical_or(xs != x, cs != c))
                    def _():
                        greet(z * 8 + xs * 2 + cs, ys)
                else:
                    greet(z * 8 + xs * 2 + cs, ys)

    greet(partner, y)

    @pl.when(has_cross)
    def _():
        greet(across, y)

    low = lax.broadcasted_iota(jnp.int32, (2, 32, 128), 2) < HEAD_DIM

    def pack(kind, first, second, scale):
        for p in range(HEADS // 2):
            one = inb[first, :, :, p * 128 : (p + 1) * 128]
            two = inb[second, :, :, p * 128 : (p + 1) * 128]
            if scale:
                one = one * jnp.bfloat16(SCALE)
            stage[kind, 2 * p] = jnp.where(low, one, turned(two))
            stage[kind, 2 * p + 1] = jnp.where(low, turned(one), two)

    loads[0].wait()
    loads[1].wait()
    pack(0, 0, 1, False)
    loads[2].wait()
    loads[3].wait()
    pack(1, 2, 3, True)

    pl.semaphore_wait(
        barrier, 17 - stays.astype(jnp.int32) + has_cross.astype(jnp.int32)
    )

    rows = pl.ds(pl.multiple_of(y * 32, 32), 32)

    def to_slab(kind, i, act):
        dx, dy = OFFSETS[i]
        xd = lax.rem(x + dx, 4)
        yd = lax.rem(y + dy, 4)
        src = stage.at[kind, yd * 4 + xd]
        if kind == 0:
            dst = win.at[pl.ds(HALO + 2 * pair, 2), rows, :]
            landed = kv_recv.at[pair, y]
        else:
            dst = own_qd.at[pl.ds(2 * pair, 2), rows, :]
            landed = qd_recv.at[pair]
        remote = pltpu.make_async_remote_copy(
            src_ref=src,
            dst_ref=dst,
            send_sem=send_sem.at[kind, i],
            recv_sem=landed,
            device_id=(z * 8 + xd * 2 + home, yd),
            device_id_type=MESH,
        )
        if dx == 0 and dy == 0:
            if act == "start":
                local = pltpu.make_async_copy(src, dst, landed)
                pl.when(stays)(local.start)
                pl.when(jnp.logical_not(stays))(remote.start)
            else:
                pl.when(jnp.logical_not(stays))(remote.wait_send)
        elif act == "start":
            remote.start()
        else:
            remote.wait_send()

    for i in range(16):
        to_slab(0, i, "start")

    for i in range(16):
        to_slab(1, i, "start")

    far = jnp.where(c == 0, 0, HALO + OWN)

    @pl.when(jnp.logical_not(has_cross))
    def _():
        win[pl.ds(far, HALO)] = jnp.zeros((HALO, TOK, 128), jnp.bfloat16)
        cross_in[...] = jnp.zeros_like(cross_in)

    def byte_wait(ref, sem):
        pltpu.make_async_copy(ref, ref, sem).wait()

    def flip(w):
        wint[w] = win[w].T

    passed = []
    for n, dy in enumerate((2, 1, 3, 0)):
        ys = lax.rem(y + dy, 4)
        some = pl.ds(pl.multiple_of(ys * 32, 32), 32)
        for k in (1, 2, 0, 3):
            here = win.at[HALO + 2 * k : HALO + 2 * k + 2, some, :]
            byte_wait(here, kv_recv.at[k, ys])
            for side, land in ((0, 2 * k - 2), (1, HALO + OWN + 2 * k)):
                if k == (0, 3)[side]:
                    continue
                copy = pltpu.make_async_remote_copy(
                    src_ref=here,
                    dst_ref=win.at[land : land + 2, some, :],
                    send_sem=halo_send.at[side, k - 1 + side, n],
                    recv_sem=halo_recv.at[side],
                    device_id=((up, down)[side], y),
                    device_id_type=MESH,
                )
                pl.when((has_up, has_down)[side])(copy.start)
                passed.append((side, copy))
    part_copy.wait()

    base = pos * OWN - HALO

    def turned_frame(i):
        return jnp.where(c == 0, i, OWN - 1 - i)

    @pl.loop(0, OWN)
    def _(i):
        f = turned_frame(i)
        at_frame = pos * OWN + f
        for w in range(WIN):
            target = base + jnp.where(c == 0, w, WIN - 1 - w)
            at = jnp.int32(ZERO)
            for s in range(SLOTS):
                at = jnp.where(part[s, at_frame] == target, i * KEYS + 1 + s, at)
            table[i, w] = jnp.where(i + HALO == w, i * KEYS, at)

    terms[ZERO] = jnp.zeros((TOK, 128), jnp.float32)
    for f in range(OWN):
        flip(HALO + f)
    for k in range(4):
        byte_wait(own_qd.at[2 * k : 2 * k + 2], qd_recv.at[k])

    @pl.when(has_down)
    def _():
        byte_wait(win.at[:HALO], halo_recv.at[0])

    @pl.when(has_up)
    def _():
        byte_wait(win.at[HALO + OWN :], halo_recv.at[1])

    for w in range(HALO):
        flip(w)
        flip(HALO + OWN + w)

    half = lax.broadcasted_iota(jnp.int32, (TOK, 128), 1) < HEAD_DIM

    def slots_of(i):
        f = turned_frame(i)
        at = [f + HALO]
        bias = [None]
        for s in range(SLOTS):
            listed = part[s, pos * OWN + f]
            close = jnp.minimum(jnp.maximum(listed - base, 0), WIN - 1)
            at.append(jnp.where(listed >= 0, close, f + HALO))
            bias.append(jnp.where(listed >= 0, jnp.float32(0.0), jnp.float32(-jnp.inf)))
        return f, at, bias

    def block_diagonal(f):
        mixed = own_qd[f]
        none = jnp.zeros_like(mixed)
        return jnp.concatenate([jnp.where(half, none, mixed), jnp.where(half, mixed, none)], axis=0)

    def products(i):
        u = i % 2
        f, at, bias = slots_of(i)
        keyed = jnp.concatenate([win[at[s]] for s in range(KEYS)], axis=0)
        both = lax.dot_general(
            keyed, block_diagonal(f), (((1,), (1,)), ((), ())), preferred_element_type=jnp.float32
        )
        top = None
        for s in range(KEYS):
            here = both[s * TOK : (s + 1) * TOK]
            score = here[:, 128:]
            if bias[s] is not None:
                score = score + bias[s]
            sc[u, s, :, :128] = here[:, :128]
            sc[u, s, :, 128:] = score
            most = jnp.max(score.reshape(16, 8, 128), axis=0)
            top = most if top is None else jnp.maximum(top, most)
        peaks[u] = top

    def exponentials(i):
        u = i % 2
        peak = jnp.max(peaks[u], axis=0, keepdims=True)
        total = jnp.zeros((8, 128), jnp.float32)
        dsum = jnp.zeros((8, 128), jnp.float32)
        for s in range(KEYS):
            e = jnp.exp(sc[u, s, :, 128:] - peak)
            sc[u, s, :, 128:] = e
            total = total + jnp.sum(e.reshape(16, 8, 128), axis=0)
            dsum = dsum + jnp.sum((e * sc[u, s, :, :128]).reshape(16, 8, 128), axis=0)
        inv = 1.0 / jnp.sum(total, axis=0, keepdims=True)
        return inv, jnp.sum(dsum, axis=0, keepdims=True) * inv

    def gradients(i, inv, delta):
        u = i % 2
        for s in range(KEYS):
            w = sc[u, s, :, 128:] * inv
            rows_at = slice(s * TOK, (s + 1) * TOK)
            pd[u, rows_at, :128] = w.astype(jnp.bfloat16)
            pd[u, rows_at, 128:] = (w * (sc[u, s, :, :128] - delta)).astype(jnp.bfloat16)

    def key_terms(i):
        u = i % 2
        prod = jnp.dot(pd[u], block_diagonal(turned_frame(i)), preferred_element_type=jnp.float32)
        for s in range(KEYS):
            terms[i * KEYS + s] = prod[s * TOK : (s + 1) * TOK]

    def query_terms(i):
        u = i % 2
        f, at, _ = slots_of(i)
        turned_kv = jnp.concatenate([wint[at[s]] for s in range(KEYS)], axis=1)
        res = jnp.dot(turned_kv, pd[u], preferred_element_type=jnp.float32)
        outcome = jnp.concatenate([res[:HEAD_DIM, 128:] * SCALE, res[HEAD_DIM:, :128]], axis=0)
        outs[0, f] = outcome.T.astype(jnp.bfloat16)

    def gathered(w):
        total = None
        for i in range(max(0, w - 2 * HALO), min(OWN, w + 1)):
            term = terms[table[i, w]]
            total = term if total is None else total + term
        return total

    def pair_of(j):
        return jnp.where(c == 0, j, 3 - j)

    def give_back(kind, j, act):
        k = pair_of(j)
        xs = 2 * c + lax.div(k, 2)
        cs = lax.rem(k, 2)
        for dy in range(4):
            ys = lax.rem(y + (2, 1, 3, 0)[dy], 4)
            src = outs.at[kind, pl.ds(2 * k, 2), pl.ds(pl.multiple_of(ys * 32, 32), 32), :]
            dst = ostage.at[kind, head]
            remote = pltpu.make_async_remote_copy(
                src_ref=src,
                dst_ref=dst,
                send_sem=out_send.at[kind, j, dy],
                recv_sem=out_recv.at[kind],
                device_id=(z * 8 + xs * 2 + cs, ys),
                device_id_type=MESH,
            )
            if dy == 3:
                mine = jnp.logical_and(xs == x, cs == c)
                if act == "start":
                    local = pltpu.make_async_copy(src, dst, out_recv.at[kind])
                    pl.when(mine)(local.start)
                    pl.when(jnp.logical_not(mine))(remote.start)
                else:
                    pl.when(jnp.logical_not(mine))(remote.wait_send)
            elif act == "start":
                remote.start()
            else:
                remote.wait_send()

    cross_copies = [
        pltpu.make_async_remote_copy(
            src_ref=cross_out.at[2 * j : 2 * j + 2],
            dst_ref=cross_in.at[2 * j : 2 * j + 2],
            send_sem=cross_send.at[j],
            recv_sem=cross_recv.at[j],
            device_id=(across, y),
            device_id_type=MESH,
        )
        for j in range(3)
    ]

    products(0)
    for i in range(OWN + 1):
        if i + 1 < OWN:
            products(i + 1)
        if i < OWN:
            inv, delta = exponentials(i)
        if i > 0:
            key_terms(i - 1)
        if i < OWN:
            gradients(i, inv, delta)
        if i > 0:
            query_terms(i - 1)
        if i > 0 and i % 2 == 0:
            j = i // 2 - 1
            if j < 3:
                for w in (2 * j, 2 * j + 1):
                    cross_out[w] = gathered(w).astype(jnp.bfloat16)
                pl.when(has_cross)(cross_copies[j].start)
            give_back(0, j, "start")

    ret_copies = []
    for j in range(3):
        for q in (2 * j, 2 * j + 1):
            die_out[q] = gathered(HALO + OWN + q).astype(jnp.bfloat16)
        copy = pltpu.make_async_remote_copy(
            src_ref=die_out.at[2 * j : 2 * j + 2],
            dst_ref=die_in.at[2 * j : 2 * j + 2],
            send_sem=ret_send.at[j],
            recv_sem=ret_recv.at[j],
            device_id=(partner, y),
            device_id_type=MESH,
        )
        copy.start()
        ret_copies.append(copy)
    for j in (0, 3, 2, 1):
        sums = [gathered(HALO + i) for i in (2 * j, 2 * j + 1)]
        if j < 3:
            pl.when(has_cross)(cross_copies[2 - j].wait_recv)
        if j > 0:
            ret_copies[3 - j].wait_recv()
        for n, i in enumerate((2 * j, 2 * j + 1)):
            total = sums[n]
            if i < HALO:
                total = total + cross_in[HALO - 1 - i].astype(jnp.float32)
            if j > 0:
                total = total + die_in[OWN - 1 - i].astype(jnp.float32)
            outs[1, turned_frame(i)] = total.astype(jnp.bfloat16)
        give_back(1, j, "start")

    for i in range(16):
        to_slab(0, i, "wait")
        to_slab(1, i, "wait")
    for side, copy in passed:
        pl.when((has_up, has_down)[side])(copy.wait_send)
    for copy in cross_copies:
        pl.when(has_cross)(copy.wait_send)
    for copy in ret_copies:
        copy.wait_send()
    for j in range(4):
        give_back(0, j, "wait")
        give_back(1, j, "wait")
    for kind in range(2):
        byte_wait(ostage.at[kind], out_recv.at[kind])


def per_device(query, keyed, valued, grad_out, partners):
    depth = lax.axis_size("frames") // 8
    dma = pltpu.SemaphoreType.DMA
    staged = pl.pallas_call(
        functools.partial(kernel, depth),
        out_shape=jax.ShapeDtypeStruct((2, HEADS, 2, 32, 128), jnp.bfloat16),
        in_specs=[pl.BlockSpec(memory_space=pltpu.HBM)] * 5,
        out_specs=pl.BlockSpec(memory_space=pltpu.HBM),
        scratch_shapes=[
            pltpu.VMEM((4, 2, 32, 1024), jnp.bfloat16),
            pltpu.VMEM((2, HEADS, 2, 32, 128), jnp.bfloat16),
            pltpu.VMEM((WIN, TOK, 128), jnp.bfloat16),
            pltpu.VMEM((WIN, 128, TOK), jnp.bfloat16),
            pltpu.VMEM((OWN, TOK, 128), jnp.bfloat16),
            pltpu.VMEM((2, KEYS, TOK, 256), jnp.float32),
            pltpu.VMEM((2, KEYS * TOK, 256), jnp.bfloat16),
            pltpu.VMEM((ZERO + 1, TOK, 128), jnp.float32),
            pltpu.VMEM((2, 8, 128), jnp.float32),
            pltpu.VMEM((HALO, TOK, 128), jnp.bfloat16),
            pltpu.VMEM((HALO, TOK, 128), jnp.bfloat16),
            pltpu.VMEM((HALO, TOK, 128), jnp.bfloat16),
            pltpu.VMEM((HALO, TOK, 128), jnp.bfloat16),
            pltpu.VMEM((2, OWN, TOK, 128), jnp.bfloat16),
            pltpu.SMEM(partners.shape[::-1], jnp.int32),
            pltpu.SMEM((OWN, WIN), jnp.int32),
            dma((4,)),
            dma(()),
            dma((2, 16)),
            dma((4, 4)),
            dma((4,)),
            dma((2, 3, 4)),
            dma((2,)),
            dma((3,)),
            dma((3,)),
            dma((3,)),
            dma((3,)),
            dma((2, 4, 4)),
            dma((2,)),
        ],
        compiler_params=pltpu.CompilerParams(collective_id=0, has_side_effects=True),
    )(query, keyed, valued, grad_out, partners.T)
    return unpacked(staged, query.shape)


def solution(mesh):
    spec = P("frames", "heads", None)
    return jax.shard_map(
        per_device,
        mesh=mesh,
        in_specs=(spec, spec, spec, spec, P()),
        out_specs=(spec,) * 4,
        check_vma=False,
    )
```

```python
import functools

import jax
import jax.numpy as jnp
from jax import lax
from jax.experimental import pallas as pl
from jax.experimental.pallas import tpu as pltpu
from jax.sharding import PartitionSpec as P

HEAD_DIM = 64
SLOTS = 6
KEYS = SLOTS + 1
HALO = 6
OWN = 8
WIN = OWN + 2 * HALO
TOK = 128
HEADS = 16
ZERO = OWN * KEYS
MESH = pl.DeviceIdType.MESH
ORDER = (6, 0, 1, 2, 3, 4, 5, 7)
SCALE = float(HEAD_DIM) ** -0.5
OFFSETS = sorted(
    [(dx, dy) for dx in range(4) for dy in range(4)],
    key=lambda o: -(min(o[0], 4 - o[0]) + min(o[1], 4 - o[1])),
)


def turned(value):
    return jnp.concatenate([value[..., HEAD_DIM:], value[..., :HEAD_DIM]], axis=-1)


def unpack_kernel(taken, att_hbm, qg_hbm, kg_hbm, vg_hbm, whole, sem):
    low = lax.broadcasted_iota(jnp.int32, (2, 32, 128), 2) < HEAD_DIM
    outs = (qg_hbm, att_hbm, kg_hbm, vg_hbm)
    copies = []
    for kind in range(2):
        for p in range(HEADS // 2):
            at = slice(p * 128, (p + 1) * 128)
            even = taken[kind, 2 * p]
            odd = taken[kind, 2 * p + 1]
            whole[2 * kind, :, :, at] = jnp.where(low, even, turned(odd))
            whole[2 * kind + 1, :, :, at] = jnp.where(low, turned(even), odd)
        for i in (2 * kind, 2 * kind + 1):
            copies.append(pltpu.make_async_copy(whole.at[i], outs[i], sem.at[i]))
            copies[-1].start()
    for copy in copies:
        copy.wait()


def unpacked(staged, shape):
    return pl.pallas_call(
        unpack_kernel,
        out_shape=(jax.ShapeDtypeStruct(shape, jnp.bfloat16),) * 4,
        in_specs=[pl.BlockSpec(memory_space=pltpu.VMEM)],
        out_specs=(pl.BlockSpec(memory_space=pltpu.HBM),) * 4,
        scratch_shapes=[
            pltpu.VMEM((4,) + shape, jnp.bfloat16),
            pltpu.SemaphoreType.DMA((4,)),
        ],
        compiler_params=pltpu.CompilerParams(vmem_limit_bytes=16 * 2**20),
    )(staged)


def kernel(
    depth,
    q_hbm,
    k_hbm,
    v_hbm,
    g_hbm,
    part_hbm,
    ostage,
    inb,
    stage,
    win,
    far_land,
    wint,
    own_qd,
    sc,
    pd,
    terms,
    peaks,
    cross_out,
    cross_in,
    die_out,
    die_in,
    outs,
    part,
    table,
    in_sem,
    part_sem,
    send_sem,
    kv_recv,
    qd_recv,
    halo_send,
    halo_recv,
    cross_send,
    cross_recv,
    ret_send,
    ret_recv,
    out_send,
    out_recv,
):
    fi = lax.axis_index("frames")
    y = lax.axis_index("heads")
    z = lax.div(fi, 8)
    x = lax.rem(lax.div(fi, 2), 4)
    c = lax.rem(fi, 2)
    pos = z * 2 + c
    head = y * 4 + x
    home = lax.div(x, 2)
    pair = lax.rem(x, 2) * 2 + c
    stays = home == c
    partner = fi + 1 - 2 * c
    up = jnp.where(c == 0, fi + 1, fi + 7)
    down = jnp.where(c == 1, fi - 1, fi - 7)
    has_up = pos < 2 * depth - 1
    has_down = pos > 0
    has_cross = jnp.logical_or(jnp.logical_and(c == 1, has_up), jnp.logical_and(c == 0, has_down))
    across = jnp.where(c == 0, down, up)

    loads = [
        pltpu.make_async_copy(ref, inb.at[i], in_sem.at[i])
        for i, ref in enumerate((k_hbm, v_hbm, q_hbm, g_hbm))
    ]
    for copy in loads:
        copy.start()
    part_copy = pltpu.make_async_copy(part_hbm, part, part_sem)
    part_copy.start()

    barrier = pltpu.get_barrier_semaphore()

    def greet(frame_at, head_at):
        pl.semaphore_signal(barrier, inc=1, device_id=(frame_at, head_at), device_id_type=MESH)

    for j in range(2):
        for cs in range(2):
            xs = 2 * c + j
            for dy in (2, 1, 3, 0):
                ys = lax.rem(y + dy, 4)
                if dy == 0:

                    @pl.when(jnp.logical_or(xs != x, cs != c))
                    def _():
                        greet(z * 8 + xs * 2 + cs, ys)
                else:
                    greet(z * 8 + xs * 2 + cs, ys)

    greet(partner, y)

    @pl.when(has_cross)
    def _():
        greet(across, y)

    low = lax.broadcasted_iota(jnp.int32, (2, 32, 128), 2) < HEAD_DIM

    def pack(kind, first, second, scale):
        for p in range(HEADS // 2):
            one = inb[first, :, :, p * 128 : (p + 1) * 128]
            two = inb[second, :, :, p * 128 : (p + 1) * 128]
            if scale:
                one = one * jnp.bfloat16(SCALE)
            stage[kind, 2 * p] = jnp.where(low, one, turned(two))
            stage[kind, 2 * p + 1] = jnp.where(low, turned(one), two)

    loads[0].wait()
    loads[1].wait()
    pack(0, 0, 1, False)

    pl.semaphore_wait(
        barrier, 17 - stays.astype(jnp.int32) + has_cross.astype(jnp.int32)
    )

    rows = pl.ds(pl.multiple_of(y * 32, 32), 32)

    def to_slab(kind, i, act):
        dx, dy = OFFSETS[i]
        xd = lax.rem(x + dx, 4)
        yd = lax.rem(y + dy, 4)
        src = stage.at[kind, yd * 4 + xd]
        if kind == 0:
            dst = win.at[pl.ds(HALO + 2 * pair, 2), rows, :]
            landed = kv_recv.at[pair, y]
        else:
            dst = own_qd.at[pl.ds(2 * pair, 2), rows, :]
            landed = qd_recv.at[pair]
        remote = pltpu.make_async_remote_copy(
            src_ref=src,
            dst_ref=dst,
            send_sem=send_sem.at[kind, i],
            recv_sem=landed,
            device_id=(z * 8 + xd * 2 + home, yd),
            device_id_type=MESH,
        )
        if dx == 0 and dy == 0:
            if act == "start":
                local = pltpu.make_async_copy(src, dst, landed)
                pl.when(stays)(local.start)
                pl.when(jnp.logical_not(stays))(remote.start)
            else:
                pl.when(jnp.logical_not(stays))(remote.wait_send)
        elif act == "start":
            remote.start()
        else:
            remote.wait_send()

    for i in range(16):
        to_slab(0, i, "start")

    loads[2].wait()
    loads[3].wait()
    pack(1, 2, 3, True)
    for i in range(16):
        to_slab(1, i, "start")

    far = jnp.where(c == 0, 0, HALO + OWN)

    @pl.when(jnp.logical_not(has_cross))
    def _():
        far_land[...] = jnp.zeros_like(far_land)
        cross_in[...] = jnp.zeros_like(cross_in)

    def byte_wait(ref, sem):
        pltpu.make_async_copy(ref, ref, sem).wait()

    def flip(w):
        wint[w] = win[w].T

    passed = []
    for n, dy in enumerate((2, 1, 3, 0)):
        ys = lax.rem(y + dy, 4)
        some = pl.ds(pl.multiple_of(ys * 32, 32), 32)
        for k in (1, 2, 0, 3):
            here = win.at[HALO + 2 * k : HALO + 2 * k + 2, some, :]
            byte_wait(here, kv_recv.at[k, ys])
            to_partner = pltpu.make_async_remote_copy(
                src_ref=here,
                dst_ref=win.at[pl.ds(jnp.where(c == 0, 2 * k - 2, HALO + OWN + 2 * k), 2), some, :],
                send_sem=halo_send.at[0, k, n],
                recv_sem=halo_recv.at[0],
                device_id=(partner, y),
                device_id_type=MESH,
            )
            to_across = pltpu.make_async_remote_copy(
                src_ref=here,
                dst_ref=far_land.at[pl.ds(jnp.where(c == 0, 2 * k, 2 * k - 2), 2), some, :],
                send_sem=halo_send.at[1, k, n],
                recv_sem=halo_recv.at[1],
                device_id=(across, y),
                device_id_type=MESH,
            )
            if k in (1, 2):
                crossing = has_cross
                to_partner.start()
                passed.append((None, to_partner))
            else:
                staying = (c == 1) if k == 0 else (c == 0)
                crossing = jnp.logical_and(has_cross, jnp.logical_not(staying))
                pl.when(staying)(to_partner.start)
                passed.append((staying, to_partner))
            pl.when(crossing)(to_across.start)
            passed.append((crossing, to_across))
    part_copy.wait()

    base = pos * OWN - HALO

    def turned_frame(i):
        return jnp.where(c == 0, i, OWN - 1 - i)

    @pl.loop(0, OWN)
    def _(i):
        f = turned_frame(i)
        at_frame = pos * OWN + f
        for w in range(WIN):
            target = base + jnp.where(c == 0, w, WIN - 1 - w)
            at = jnp.int32(ZERO)
            for s in range(SLOTS):
                at = jnp.where(part[s, at_frame] == target, i * KEYS + 1 + s, at)
            table[i, w] = jnp.where(i + HALO == w, i * KEYS, at)

    terms[ZERO] = jnp.zeros((TOK, 128), jnp.float32)
    for f in range(OWN):
        flip(HALO + f)
    for k in range(4):
        byte_wait(own_qd.at[2 * k : 2 * k + 2], qd_recv.at[k])

    near = jnp.where(c == 0, HALO + OWN, 0)
    byte_wait(win.at[pl.ds(near, HALO)], halo_recv.at[0])
    for w in range(HALO):
        flip(near + w)

    half = lax.broadcasted_iota(jnp.int32, (TOK, 128), 1) < HEAD_DIM

    def slots_of(i):
        f = turned_frame(i)
        at = [f + HALO]
        bias = [None]
        for s in range(SLOTS):
            listed = part[s, pos * OWN + f]
            close = jnp.minimum(jnp.maximum(listed - base, 0), WIN - 1)
            at.append(jnp.where(listed >= 0, close, f + HALO))
            bias.append(jnp.where(listed >= 0, jnp.float32(0.0), jnp.float32(-jnp.inf)))
        return f, at, bias

    def block_diagonal(f):
        mixed = own_qd[f]
        none = jnp.zeros_like(mixed)
        return jnp.concatenate([jnp.where(half, none, mixed), jnp.where(half, mixed, none)], axis=0)

    def products(n):
        u = n % 2
        f, at, bias = slots_of(ORDER[n])
        keyed = jnp.concatenate([win[at[s]] for s in range(KEYS)], axis=0)
        both = lax.dot_general(
            keyed, block_diagonal(f), (((1,), (1,)), ((), ())), preferred_element_type=jnp.float32
        )
        top = None
        for s in range(KEYS):
            here = both[s * TOK : (s + 1) * TOK]
            score = here[:, 128:]
            if bias[s] is not None:
                score = score + bias[s]
            sc[u, s, :, :128] = here[:, :128]
            sc[u, s, :, 128:] = score
            most = jnp.max(score.reshape(16, 8, 128), axis=0)
            top = most if top is None else jnp.maximum(top, most)
        peaks[u] = top

    def exponentials(n):
        u = n % 2
        peak = jnp.max(peaks[u], axis=0, keepdims=True)
        total = jnp.zeros((8, 128), jnp.float32)
        dsum = jnp.zeros((8, 128), jnp.float32)
        for s in range(KEYS):
            e = jnp.exp(sc[u, s, :, 128:] - peak)
            sc[u, s, :, 128:] = e
            total = total + jnp.sum(e.reshape(16, 8, 128), axis=0)
            dsum = dsum + jnp.sum((e * sc[u, s, :, :128]).reshape(16, 8, 128), axis=0)
        inv = 1.0 / jnp.sum(total, axis=0, keepdims=True)
        return inv, jnp.sum(dsum, axis=0, keepdims=True) * inv

    def gradients(n, inv, delta):
        u = n % 2
        for s in range(KEYS):
            w = sc[u, s, :, 128:] * inv
            rows_at = slice(s * TOK, (s + 1) * TOK)
            pd[u, rows_at, :128] = w.astype(jnp.bfloat16)
            pd[u, rows_at, 128:] = (w * (sc[u, s, :, :128] - delta)).astype(jnp.bfloat16)

    def key_terms(n):
        u = n % 2
        prod = jnp.dot(pd[u], block_diagonal(turned_frame(ORDER[n])), preferred_element_type=jnp.float32)
        for s in range(KEYS):
            terms[ORDER[n] * KEYS + s] = prod[s * TOK : (s + 1) * TOK]

    def query_terms(n):
        u = n % 2
        f, at, _ = slots_of(ORDER[n])
        turned_kv = jnp.concatenate([wint[at[s]] for s in range(KEYS)], axis=1)
        res = jnp.dot(turned_kv, pd[u], preferred_element_type=jnp.float32)
        outcome = jnp.concatenate([res[:HEAD_DIM, 128:] * SCALE, res[HEAD_DIM:, :128]], axis=0)
        outs[0, f] = outcome.T.astype(jnp.bfloat16)

    def gathered(w):
        total = None
        for i in range(max(0, w - 2 * HALO), min(OWN, w + 1)):
            term = terms[table[i, w]]
            total = term if total is None else total + term
        return total

    def pair_of(j):
        return jnp.where(c == 0, j, 3 - j)

    def give_back(kind, j, act):
        k = pair_of(j)
        xs = 2 * c + lax.div(k, 2)
        cs = lax.rem(k, 2)
        for dy in range(4):
            ys = lax.rem(y + (2, 1, 3, 0)[dy], 4)
            src = outs.at[kind, pl.ds(2 * k, 2), pl.ds(pl.multiple_of(ys * 32, 32), 32), :]
            dst = ostage.at[kind, head]
            remote = pltpu.make_async_remote_copy(
                src_ref=src,
                dst_ref=dst,
                send_sem=out_send.at[kind, j, dy],
                recv_sem=out_recv.at[kind],
                device_id=(z * 8 + xs * 2 + cs, ys),
                device_id_type=MESH,
            )
            if dy == 3:
                mine = jnp.logical_and(xs == x, cs == c)
                if act == "start":
                    local = pltpu.make_async_copy(src, dst, out_recv.at[kind])
                    pl.when(mine)(local.start)
                    pl.when(jnp.logical_not(mine))(remote.start)
                else:
                    pl.when(jnp.logical_not(mine))(remote.wait_send)
            elif act == "start":
                remote.start()
            else:
                remote.wait_send()

    cross_copies = [
        pltpu.make_async_remote_copy(
            src_ref=cross_out.at[2 * j : 2 * j + 2],
            dst_ref=cross_in.at[2 * j : 2 * j + 2],
            send_sem=cross_send.at[j],
            recv_sem=cross_recv.at[j],
            device_id=(across, y),
            device_id_type=MESH,
        )
        for j in range(3)
    ]

    products(0)

    @pl.when(has_cross)
    def _():
        byte_wait(far_land, halo_recv.at[1])

    for w in range(HALO):
        win[far + w] = far_land[w]
        wint[far + w] = far_land[w].T

    for n in range(OWN + 1):
        if n + 1 < OWN:
            products(n + 1)
        if n < OWN:
            inv, delta = exponentials(n)
        if n > 0:
            key_terms(n - 1)
        if n < OWN:
            gradients(n, inv, delta)
        if n > 0:
            query_terms(n - 1)
        if n in (3, 5, 7, 8):
            j = (3, 5, 7, 8).index(n)
            if j < 3:
                for w in (2 * j, 2 * j + 1):
                    cross_out[w] = gathered(w).astype(jnp.bfloat16)
                pl.when(has_cross)(cross_copies[j].start)
            give_back(0, j, "start")

    ret_copies = []
    for j in range(3):
        for q in (2 * j, 2 * j + 1):
            die_out[q] = gathered(HALO + OWN + q).astype(jnp.bfloat16)
        copy = pltpu.make_async_remote_copy(
            src_ref=die_out.at[2 * j : 2 * j + 2],
            dst_ref=die_in.at[2 * j : 2 * j + 2],
            send_sem=ret_send.at[j],
            recv_sem=ret_recv.at[j],
            device_id=(partner, y),
            device_id_type=MESH,
        )
        copy.start()
        ret_copies.append(copy)
    for j in (3, 2, 1, 0):
        sums = [gathered(HALO + i) for i in (2 * j, 2 * j + 1)]
        if j < 3:
            pl.when(has_cross)(cross_copies[2 - j].wait_recv)
        if j > 0:
            ret_copies[3 - j].wait_recv()
        for n, i in enumerate((2 * j, 2 * j + 1)):
            total = sums[n]
            if i < HALO:
                total = total + cross_in[HALO - 1 - i].astype(jnp.float32)
            if j > 0:
                total = total + die_in[OWN - 1 - i].astype(jnp.float32)
            outs[1, turned_frame(i)] = total.astype(jnp.bfloat16)
        give_back(1, j, "start")

    for i in range(16):
        to_slab(0, i, "wait")
        to_slab(1, i, "wait")
    for wanted, copy in passed:
        if wanted is None:
            copy.wait_send()
        else:
            pl.when(wanted)(copy.wait_send)
    for copy in cross_copies:
        pl.when(has_cross)(copy.wait_send)
    for copy in ret_copies:
        copy.wait_send()
    for j in range(4):
        give_back(0, j, "wait")
        give_back(1, j, "wait")
    for kind in range(2):
        byte_wait(ostage.at[kind], out_recv.at[kind])


def per_device(query, keyed, valued, grad_out, partners):
    depth = lax.axis_size("frames") // 8
    dma = pltpu.SemaphoreType.DMA
    staged = pl.pallas_call(
        functools.partial(kernel, depth),
        out_shape=pltpu.VMEM((2, HEADS, 2, 32, 128), jnp.bfloat16),
        in_specs=[pl.BlockSpec(memory_space=pltpu.HBM)] * 5,
        out_specs=pl.BlockSpec(memory_space=pltpu.VMEM),
        scratch_shapes=[
            pltpu.VMEM((4, 2, 32, 1024), jnp.bfloat16),
            pltpu.VMEM((2, HEADS, 2, 32, 128), jnp.bfloat16),
            pltpu.VMEM((WIN, TOK, 128), jnp.bfloat16),
            pltpu.VMEM((HALO, TOK, 128), jnp.bfloat16),
            pltpu.VMEM((WIN, 128, TOK), jnp.bfloat16),
            pltpu.VMEM((OWN, TOK, 128), jnp.bfloat16),
            pltpu.VMEM((2, KEYS, TOK, 256), jnp.float32),
            pltpu.VMEM((2, KEYS * TOK, 256), jnp.bfloat16),
            pltpu.VMEM((ZERO + 1, TOK, 128), jnp.float32),
            pltpu.VMEM((2, 8, 128), jnp.float32),
            pltpu.VMEM((HALO, TOK, 128), jnp.bfloat16),
            pltpu.VMEM((HALO, TOK, 128), jnp.bfloat16),
            pltpu.VMEM((HALO, TOK, 128), jnp.bfloat16),
            pltpu.VMEM((HALO, TOK, 128), jnp.bfloat16),
            pltpu.VMEM((2, OWN, TOK, 128), jnp.bfloat16),
            pltpu.SMEM(partners.shape[::-1], jnp.int32),
            pltpu.SMEM((OWN, WIN), jnp.int32),
            dma((4,)),
            dma(()),
            dma((2, 16)),
            dma((4, 4)),
            dma((4,)),
            dma((2, 4, 4)),
            dma((2,)),
            dma((3,)),
            dma((3,)),
            dma((3,)),
            dma((3,)),
            dma((2, 4, 4)),
            dma((2,)),
        ],
        compiler_params=pltpu.CompilerParams(collective_id=0, has_side_effects=True, vmem_limit_bytes=60 * 2**20),
    )(query, keyed, valued, grad_out, partners.T)
    return unpacked(staged, query.shape)


def solution(mesh):
    spec = P("frames", "heads", None)
    return jax.shard_map(
        per_device,
        mesh=mesh,
        in_specs=(spec, spec, spec, spec, P()),
        out_specs=(spec,) * 4,
        check_vma=False,
    )
```

```python
import functools

import jax
import jax.numpy as jnp
from jax import lax
from jax.experimental import pallas as pl
from jax.experimental.pallas import tpu as pltpu
from jax.sharding import PartitionSpec as P

HEAD_DIM = 64
SLOTS = 6
KEYS = SLOTS + 1
HALO = 6
OWN = 8
WIN = OWN + 2 * HALO
TOK = 128
HEADS = 16
ZERO = OWN * KEYS
MESH = pl.DeviceIdType.MESH
ORDER = (6, 0, 1, 2, 3, 4, 5, 7)
SCALE = float(HEAD_DIM) ** -0.5
OFFSETS = sorted(
    [(dx, dy) for dx in range(4) for dy in range(4)],
    key=lambda o: -(min(o[0], 4 - o[0]) + min(o[1], 4 - o[1])),
)


def turned(value):
    return jnp.concatenate([value[..., HEAD_DIM:], value[..., :HEAD_DIM]], axis=-1)


def unpack_kernel(taken, att_hbm, qg_hbm, kg_hbm, vg_hbm, whole, sem):
    low = lax.broadcasted_iota(jnp.int32, (2, 32, 128), 2) < HEAD_DIM
    outs = (qg_hbm, att_hbm, kg_hbm, vg_hbm)
    copies = []
    for kind in range(2):
        for p in range(HEADS // 2):
            at = slice(p * 128, (p + 1) * 128)
            even = taken[kind, 2 * p]
            odd = taken[kind, 2 * p + 1]
            whole[2 * kind, :, :, at] = jnp.where(low, even, turned(odd))
            whole[2 * kind + 1, :, :, at] = jnp.where(low, turned(even), odd)
        for i in (2 * kind, 2 * kind + 1):
            copies.append(pltpu.make_async_copy(whole.at[i], outs[i], sem.at[i]))
            copies[-1].start()
    for copy in copies:
        copy.wait()


def unpacked(staged, shape):
    return pl.pallas_call(
        unpack_kernel,
        out_shape=(jax.ShapeDtypeStruct(shape, jnp.bfloat16),) * 4,
        in_specs=[pl.BlockSpec(memory_space=pltpu.VMEM)],
        out_specs=(pl.BlockSpec(memory_space=pltpu.HBM),) * 4,
        scratch_shapes=[
            pltpu.VMEM((4,) + shape, jnp.bfloat16),
            pltpu.SemaphoreType.DMA((4,)),
        ],
        compiler_params=pltpu.CompilerParams(vmem_limit_bytes=16 * 2**20),
    )(staged)


def kernel(
    depth,
    q_hbm,
    k_hbm,
    v_hbm,
    g_hbm,
    part_hbm,
    ostage,
    inb,
    stage,
    win,
    far_land,
    wint,
    own_qd,
    sc,
    pd,
    terms,
    peaks,
    cross_out,
    cross_in,
    die_out,
    die_in,
    outs,
    part,
    table,
    in_sem,
    part_sem,
    send_sem,
    kv_recv,
    qd_recv,
    halo_send,
    halo_recv,
    cross_send,
    cross_recv,
    ret_send,
    ret_recv,
    out_send,
    out_recv,
):
    fi = lax.axis_index("frames")
    y = lax.axis_index("heads")
    z = lax.div(fi, 8)
    x = lax.rem(lax.div(fi, 2), 4)
    c = lax.rem(fi, 2)
    pos = z * 2 + c
    head = y * 4 + x
    home = lax.div(x, 2)
    pair = lax.rem(x, 2) * 2 + c
    stays = home == c
    partner = fi + 1 - 2 * c
    up = jnp.where(c == 0, fi + 1, fi + 7)
    down = jnp.where(c == 1, fi - 1, fi - 7)
    has_up = pos < 2 * depth - 1
    has_down = pos > 0
    has_cross = jnp.logical_or(jnp.logical_and(c == 1, has_up), jnp.logical_and(c == 0, has_down))
    across = jnp.where(c == 0, down, up)

    loads = [
        pltpu.make_async_copy(ref, inb.at[i], in_sem.at[i])
        for i, ref in enumerate((k_hbm, v_hbm, q_hbm, g_hbm))
    ]
    for copy in loads:
        copy.start()
    part_copy = pltpu.make_async_copy(part_hbm, part, part_sem)
    part_copy.start()

    barrier = pltpu.get_barrier_semaphore()

    def greet(frame_at, head_at):
        pl.semaphore_signal(barrier, inc=1, device_id=(frame_at, head_at), device_id_type=MESH)

    for j in range(2):
        for cs in range(2):
            xs = 2 * c + j
            for dy in (2, 1, 3, 0):
                ys = lax.rem(y + dy, 4)
                if dy == 0:

                    @pl.when(jnp.logical_or(xs != x, cs != c))
                    def _():
                        greet(z * 8 + xs * 2 + cs, ys)
                else:
                    greet(z * 8 + xs * 2 + cs, ys)

    greet(partner, y)

    @pl.when(has_cross)
    def _():
        greet(across, y)

    low = lax.broadcasted_iota(jnp.int32, (2, 32, 128), 2) < HEAD_DIM

    def pack(kind, first, second, scale):
        for p in range(HEADS // 2):
            one = inb[first, :, :, p * 128 : (p + 1) * 128]
            two = inb[second, :, :, p * 128 : (p + 1) * 128]
            if scale:
                one = one * jnp.bfloat16(SCALE)
            stage[kind, 2 * p] = jnp.where(low, one, turned(two))
            stage[kind, 2 * p + 1] = jnp.where(low, turned(one), two)

    loads[0].wait()
    loads[1].wait()
    pack(0, 0, 1, False)

    pl.semaphore_wait(
        barrier, 17 - stays.astype(jnp.int32) + has_cross.astype(jnp.int32)
    )

    rows = pl.ds(pl.multiple_of(y * 32, 32), 32)

    def to_slab(kind, i, act):
        dx, dy = OFFSETS[i]
        xd = lax.rem(x + dx, 4)
        yd = lax.rem(y + dy, 4)
        src = stage.at[kind, yd * 4 + xd]
        if kind == 0:
            dst = win.at[pl.ds(HALO + 2 * pair, 2), rows, :]
            landed = kv_recv.at[pair]
        else:
            dst = own_qd.at[pl.ds(2 * pair, 2), rows, :]
            landed = qd_recv.at[pair]
        remote = pltpu.make_async_remote_copy(
            src_ref=src,
            dst_ref=dst,
            send_sem=send_sem.at[kind, i],
            recv_sem=landed,
            device_id=(z * 8 + xd * 2 + home, yd),
            device_id_type=MESH,
        )
        if dx == 0 and dy == 0:
            if act == "start":
                local = pltpu.make_async_copy(src, dst, landed)
                pl.when(stays)(local.start)
                pl.when(jnp.logical_not(stays))(remote.start)
            else:
                pl.when(jnp.logical_not(stays))(remote.wait_send)
        elif act == "start":
            remote.start()
        else:
            remote.wait_send()

    for i in range(16):
        to_slab(0, i, "start")

    loads[2].wait()
    loads[3].wait()
    pack(1, 2, 3, True)
    for i in range(16):
        to_slab(1, i, "start")

    far = jnp.where(c == 0, 0, HALO + OWN)

    @pl.when(jnp.logical_not(has_cross))
    def _():
        far_land[...] = jnp.zeros_like(far_land)
        cross_in[...] = jnp.zeros_like(cross_in)

    def byte_wait(ref, sem):
        pltpu.make_async_copy(ref, ref, sem).wait()

    def flip(w):
        wint[w] = win[w].T

    passed = []
    for k in (1, 2, 0, 3):
        here = win.at[HALO + 2 * k : HALO + 2 * k + 2]
        byte_wait(here, kv_recv.at[k])
        to_partner = pltpu.make_async_remote_copy(
            src_ref=here,
            dst_ref=win.at[pl.ds(jnp.where(c == 0, 2 * k - 2, HALO + OWN + 2 * k), 2)],
            send_sem=halo_send.at[0, k],
            recv_sem=halo_recv.at[0],
            device_id=(partner, y),
            device_id_type=MESH,
        )
        to_across = pltpu.make_async_remote_copy(
            src_ref=here,
            dst_ref=far_land.at[pl.ds(jnp.where(c == 0, 2 * k, 2 * k - 2), 2)],
            send_sem=halo_send.at[1, k],
            recv_sem=halo_recv.at[1],
            device_id=(across, y),
            device_id_type=MESH,
        )
        if k in (1, 2):
            crossing = has_cross
            to_partner.start()
            passed.append((None, to_partner))
        else:
            staying = (c == 1) if k == 0 else (c == 0)
            crossing = jnp.logical_and(has_cross, jnp.logical_not(staying))
            pl.when(staying)(to_partner.start)
            passed.append((staying, to_partner))
        pl.when(crossing)(to_across.start)
        passed.append((crossing, to_across))
    part_copy.wait()

    base = pos * OWN - HALO

    def turned_frame(i):
        return jnp.where(c == 0, i, OWN - 1 - i)

    @pl.loop(0, OWN)
    def _(i):
        f = turned_frame(i)
        at_frame = pos * OWN + f
        for w in range(WIN):
            target = base + jnp.where(c == 0, w, WIN - 1 - w)
            at = jnp.int32(ZERO)
            for s in range(SLOTS):
                at = jnp.where(part[s, at_frame] == target, i * KEYS + 1 + s, at)
            table[i, w] = jnp.where(i + HALO == w, i * KEYS, at)

    terms[ZERO] = jnp.zeros((TOK, 128), jnp.float32)
    for f in range(OWN):
        flip(HALO + f)
    for k in range(4):
        byte_wait(own_qd.at[2 * k : 2 * k + 2], qd_recv.at[k])

    near = jnp.where(c == 0, HALO + OWN, 0)
    byte_wait(win.at[pl.ds(near, HALO)], halo_recv.at[0])
    for w in range(HALO):
        flip(near + w)

    half = lax.broadcasted_iota(jnp.int32, (TOK, 128), 1) < HEAD_DIM

    def slots_of(i):
        f = turned_frame(i)
        at = [f + HALO]
        bias = [None]
        for s in range(SLOTS):
            listed = part[s, pos * OWN + f]
            close = jnp.minimum(jnp.maximum(listed - base, 0), WIN - 1)
            at.append(jnp.where(listed >= 0, close, f + HALO))
            bias.append(jnp.where(listed >= 0, jnp.float32(0.0), jnp.float32(-jnp.inf)))
        return f, at, bias

    def block_diagonal(f):
        mixed = own_qd[f]
        none = jnp.zeros_like(mixed)
        return jnp.concatenate([jnp.where(half, none, mixed), jnp.where(half, mixed, none)], axis=0)

    def products(n):
        u = n % 2
        f, at, bias = slots_of(ORDER[n])
        keyed = jnp.concatenate([win[at[s]] for s in range(KEYS)], axis=0)
        both = lax.dot_general(
            keyed, block_diagonal(f), (((1,), (1,)), ((), ())), preferred_element_type=jnp.float32
        )
        top = None
        for s in range(KEYS):
            here = both[s * TOK : (s + 1) * TOK]
            score = here[:, 128:]
            if bias[s] is not None:
                score = score + bias[s]
            sc[u, s, :, :128] = here[:, :128]
            sc[u, s, :, 128:] = score
            most = jnp.max(score.reshape(16, 8, 128), axis=0)
            top = most if top is None else jnp.maximum(top, most)
        peaks[u] = top

    def exponentials(n):
        u = n % 2
        peak = jnp.max(peaks[u], axis=0, keepdims=True)
        total = jnp.zeros((8, 128), jnp.float32)
        dsum = jnp.zeros((8, 128), jnp.float32)
        for s in range(KEYS):
            e = jnp.exp(sc[u, s, :, 128:] - peak)
            sc[u, s, :, 128:] = e
            total = total + jnp.sum(e.reshape(16, 8, 128), axis=0)
            dsum = dsum + jnp.sum((e * sc[u, s, :, :128]).reshape(16, 8, 128), axis=0)
        inv = 1.0 / jnp.sum(total, axis=0, keepdims=True)
        return inv, jnp.sum(dsum, axis=0, keepdims=True) * inv

    def gradients(n, inv, delta):
        u = n % 2
        for s in range(KEYS):
            w = sc[u, s, :, 128:] * inv
            rows_at = slice(s * TOK, (s + 1) * TOK)
            pd[u, rows_at, :128] = w.astype(jnp.bfloat16)
            pd[u, rows_at, 128:] = (w * (sc[u, s, :, :128] - delta)).astype(jnp.bfloat16)

    def key_terms(n):
        u = n % 2
        prod = jnp.dot(pd[u], block_diagonal(turned_frame(ORDER[n])), preferred_element_type=jnp.float32)
        for s in range(KEYS):
            terms[ORDER[n] * KEYS + s] = prod[s * TOK : (s + 1) * TOK]

    def query_terms(n):
        u = n % 2
        f, at, _ = slots_of(ORDER[n])
        turned_kv = jnp.concatenate([wint[at[s]] for s in range(KEYS)], axis=1)
        res = jnp.dot(turned_kv, pd[u], preferred_element_type=jnp.float32)
        outcome = jnp.concatenate([res[:HEAD_DIM, 128:] * SCALE, res[HEAD_DIM:, :128]], axis=0)
        outs[0, f] = outcome.T.astype(jnp.bfloat16)

    def gathered(w):
        total = None
        for i in range(max(0, w - 2 * HALO), min(OWN, w + 1)):
            term = terms[table[i, w]]
            total = term if total is None else total + term
        return total

    def pair_of(j):
        return jnp.where(c == 0, j, 3 - j)

    def give_back(kind, j, act):
        k = pair_of(j)
        xs = 2 * c + lax.div(k, 2)
        cs = lax.rem(k, 2)
        for dy in range(4):
            ys = lax.rem(y + (2, 1, 3, 0)[dy], 4)
            src = outs.at[kind, pl.ds(2 * k, 2), pl.ds(pl.multiple_of(ys * 32, 32), 32), :]
            dst = ostage.at[kind, head]
            remote = pltpu.make_async_remote_copy(
                src_ref=src,
                dst_ref=dst,
                send_sem=out_send.at[kind, j, dy],
                recv_sem=out_recv.at[kind],
                device_id=(z * 8 + xs * 2 + cs, ys),
                device_id_type=MESH,
            )
            if dy == 3:
                mine = jnp.logical_and(xs == x, cs == c)
                if act == "start":
                    local = pltpu.make_async_copy(src, dst, out_recv.at[kind])
                    pl.when(mine)(local.start)
                    pl.when(jnp.logical_not(mine))(remote.start)
                else:
                    pl.when(jnp.logical_not(mine))(remote.wait_send)
            elif act == "start":
                remote.start()
            else:
                remote.wait_send()

    cross_copies = [
        pltpu.make_async_remote_copy(
            src_ref=cross_out.at[2 * j : 2 * j + 2],
            dst_ref=cross_in.at[2 * j : 2 * j + 2],
            send_sem=cross_send.at[j],
            recv_sem=cross_recv.at[j],
            device_id=(across, y),
            device_id_type=MESH,
        )
        for j in range(3)
    ]

    products(0)

    @pl.when(has_cross)
    def _():
        byte_wait(far_land, halo_recv.at[1])

    for w in range(HALO):
        win[far + w] = far_land[w]
        wint[far + w] = far_land[w].T

    for n in range(OWN + 1):
        if n + 1 < OWN:
            products(n + 1)
        if n < OWN:
            inv, delta = exponentials(n)
        if n > 0:
            key_terms(n - 1)
        if n < OWN:
            gradients(n, inv, delta)
        if n > 0:
            query_terms(n - 1)
        if n in (3, 5, 7, 8):
            j = (3, 5, 7, 8).index(n)
            if j < 3:
                for w in (2 * j, 2 * j + 1):
                    cross_out[w] = gathered(w).astype(jnp.bfloat16)
                pl.when(has_cross)(cross_copies[j].start)
            give_back(0, j, "start")

    ret_copies = []
    for j in range(3):
        for q in (2 * j, 2 * j + 1):
            die_out[q] = gathered(HALO + OWN + q).astype(jnp.bfloat16)
        copy = pltpu.make_async_remote_copy(
            src_ref=die_out.at[2 * j : 2 * j + 2],
            dst_ref=die_in.at[2 * j : 2 * j + 2],
            send_sem=ret_send.at[j],
            recv_sem=ret_recv.at[j],
            device_id=(partner, y),
            device_id_type=MESH,
        )
        copy.start()
        ret_copies.append(copy)
    for j in (3, 2, 1, 0):
        sums = [gathered(HALO + i) for i in (2 * j, 2 * j + 1)]
        if j < 3:
            pl.when(has_cross)(cross_copies[2 - j].wait_recv)
        if j > 0:
            ret_copies[3 - j].wait_recv()
        for n, i in enumerate((2 * j, 2 * j + 1)):
            total = sums[n]
            if i < HALO:
                total = total + cross_in[HALO - 1 - i].astype(jnp.float32)
            if j > 0:
                total = total + die_in[OWN - 1 - i].astype(jnp.float32)
            outs[1, turned_frame(i)] = total.astype(jnp.bfloat16)
        give_back(1, j, "start")

    for i in range(16):
        to_slab(0, i, "wait")
        to_slab(1, i, "wait")
    for wanted, copy in passed:
        if wanted is None:
            copy.wait_send()
        else:
            pl.when(wanted)(copy.wait_send)
    for copy in cross_copies:
        pl.when(has_cross)(copy.wait_send)
    for copy in ret_copies:
        copy.wait_send()
    for j in range(4):
        give_back(0, j, "wait")
        give_back(1, j, "wait")
    for kind in range(2):
        byte_wait(ostage.at[kind], out_recv.at[kind])


def per_device(query, keyed, valued, grad_out, partners):
    depth = lax.axis_size("frames") // 8
    dma = pltpu.SemaphoreType.DMA
    staged = pl.pallas_call(
        functools.partial(kernel, depth),
        out_shape=pltpu.VMEM((2, HEADS, 2, 32, 128), jnp.bfloat16),
        in_specs=[pl.BlockSpec(memory_space=pltpu.HBM)] * 5,
        out_specs=pl.BlockSpec(memory_space=pltpu.VMEM),
        scratch_shapes=[
            pltpu.VMEM((4, 2, 32, 1024), jnp.bfloat16),
            pltpu.VMEM((2, HEADS, 2, 32, 128), jnp.bfloat16),
            pltpu.VMEM((WIN, TOK, 128), jnp.bfloat16),
            pltpu.VMEM((HALO, TOK, 128), jnp.bfloat16),
            pltpu.VMEM((WIN, 128, TOK), jnp.bfloat16),
            pltpu.VMEM((OWN, TOK, 128), jnp.bfloat16),
            pltpu.VMEM((2, KEYS, TOK, 256), jnp.float32),
            pltpu.VMEM((2, KEYS * TOK, 256), jnp.bfloat16),
            pltpu.VMEM((ZERO + 1, TOK, 128), jnp.float32),
            pltpu.VMEM((2, 8, 128), jnp.float32),
            pltpu.VMEM((HALO, TOK, 128), jnp.bfloat16),
            pltpu.VMEM((HALO, TOK, 128), jnp.bfloat16),
            pltpu.VMEM((HALO, TOK, 128), jnp.bfloat16),
            pltpu.VMEM((HALO, TOK, 128), jnp.bfloat16),
            pltpu.VMEM((2, OWN, TOK, 128), jnp.bfloat16),
            pltpu.SMEM(partners.shape[::-1], jnp.int32),
            pltpu.SMEM((OWN, WIN), jnp.int32),
            dma((4,)),
            dma(()),
            dma((2, 16)),
            dma((4,)),
            dma((4,)),
            dma((2, 4)),
            dma((2,)),
            dma((3,)),
            dma((3,)),
            dma((3,)),
            dma((3,)),
            dma((2, 4, 4)),
            dma((2,)),
        ],
        compiler_params=pltpu.CompilerParams(collective_id=0, has_side_effects=True, vmem_limit_bytes=60 * 2**20),
    )(query, keyed, valued, grad_out, partners.T)
    return unpacked(staged, query.shape)


def solution(mesh):
    spec = P("frames", "heads", None)
    return jax.shard_map(
        per_device,
        mesh=mesh,
        in_specs=(spec, spec, spec, spec, P()),
        out_specs=(spec,) * 4,
        check_vma=False,
    )
```

```python
import functools

import jax
import jax.numpy as jnp
from jax import lax
from jax.experimental import pallas as pl
from jax.experimental.pallas import tpu as pltpu
from jax.sharding import PartitionSpec as P

HEAD_DIM = 64
SLOTS = 6
KEYS = SLOTS + 1
HALO = 6
OWN = 8
WIN = OWN + 2 * HALO
TOK = 128
HEADS = 16
ZERO = OWN * KEYS
MESH = pl.DeviceIdType.MESH
ORDER = (6, 0, 1, 2, 3, 4, 5, 7)
SCALE = float(HEAD_DIM) ** -0.5
OFFSETS = sorted(
    [(dx, dy) for dx in range(4) for dy in range(4)],
    key=lambda o: -(min(o[0], 4 - o[0]) + min(o[1], 4 - o[1])),
)


def turned(value):
    return jnp.concatenate([value[..., HEAD_DIM:], value[..., :HEAD_DIM]], axis=-1)


def unpack_kernel(taken, att_hbm, qg_hbm, kg_hbm, vg_hbm, whole, sem):
    low = lax.broadcasted_iota(jnp.int32, (2, 32, 128), 2) < HEAD_DIM
    outs = (qg_hbm, att_hbm, kg_hbm, vg_hbm)
    copies = []
    for kind in range(2):
        for p in range(HEADS // 2):
            at = slice(p * 128, (p + 1) * 128)
            even = taken[kind, 2 * p]
            odd = taken[kind, 2 * p + 1]
            whole[2 * kind, :, :, at] = jnp.where(low, even, turned(odd))
            whole[2 * kind + 1, :, :, at] = jnp.where(low, turned(even), odd)
        for i in (2 * kind, 2 * kind + 1):
            copies.append(pltpu.make_async_copy(whole.at[i], outs[i], sem.at[i]))
            copies[-1].start()
    for copy in copies:
        copy.wait()


def unpacked(staged, shape):
    return pl.pallas_call(
        unpack_kernel,
        out_shape=(jax.ShapeDtypeStruct(shape, jnp.bfloat16),) * 4,
        in_specs=[pl.BlockSpec(memory_space=pltpu.VMEM)],
        out_specs=(pl.BlockSpec(memory_space=pltpu.HBM),) * 4,
        scratch_shapes=[
            pltpu.VMEM((4,) + shape, jnp.bfloat16),
            pltpu.SemaphoreType.DMA((4,)),
        ],
        compiler_params=pltpu.CompilerParams(vmem_limit_bytes=16 * 2**20),
    )(staged)


def kernel(
    depth,
    q_hbm,
    k_hbm,
    v_hbm,
    g_hbm,
    part_hbm,
    ostage,
    inb,
    stage,
    win,
    far_land,
    wint,
    own_qd,
    sc,
    pd,
    terms,
    peaks,
    acc,
    cross_out,
    cross_in,
    die_out,
    die_in,
    outs,
    part,
    table,
    in_sem,
    part_sem,
    send_sem,
    kv_recv,
    qd_recv,
    halo_send,
    halo_recv,
    cross_send,
    cross_recv,
    ret_send,
    ret_recv,
    out_send,
    out_recv,
):
    fi = lax.axis_index("frames")
    y = lax.axis_index("heads")
    z = lax.div(fi, 8)
    x = lax.rem(lax.div(fi, 2), 4)
    c = lax.rem(fi, 2)
    pos = z * 2 + c
    head = y * 4 + x
    home = lax.div(x, 2)
    pair = lax.rem(x, 2) * 2 + c
    stays = home == c
    partner = fi + 1 - 2 * c
    up = jnp.where(c == 0, fi + 1, fi + 7)
    down = jnp.where(c == 1, fi - 1, fi - 7)
    has_up = pos < 2 * depth - 1
    has_down = pos > 0
    has_cross = jnp.logical_or(jnp.logical_and(c == 1, has_up), jnp.logical_and(c == 0, has_down))
    across = jnp.where(c == 0, down, up)

    loads = [
        pltpu.make_async_copy(ref, inb.at[i], in_sem.at[i])
        for i, ref in enumerate((k_hbm, v_hbm, q_hbm, g_hbm))
    ]
    for copy in loads:
        copy.start()
    part_copy = pltpu.make_async_copy(part_hbm, part, part_sem)
    part_copy.start()

    barrier = pltpu.get_barrier_semaphore()

    def greet(frame_at, head_at):
        pl.semaphore_signal(barrier, inc=1, device_id=(frame_at, head_at), device_id_type=MESH)

    for j in range(2):
        for cs in range(2):
            xs = 2 * c + j
            for dy in (2, 1, 3, 0):
                ys = lax.rem(y + dy, 4)
                if dy == 0:

                    @pl.when(jnp.logical_or(xs != x, cs != c))
                    def _():
                        greet(z * 8 + xs * 2 + cs, ys)
                else:
                    greet(z * 8 + xs * 2 + cs, ys)

    greet(partner, y)

    @pl.when(has_cross)
    def _():
        greet(across, y)

    low = lax.broadcasted_iota(jnp.int32, (2, 32, 128), 2) < HEAD_DIM

    def pack(kind, first, second, scale):
        for p in range(HEADS // 2):
            one = inb[first, :, :, p * 128 : (p + 1) * 128]
            two = inb[second, :, :, p * 128 : (p + 1) * 128]
            if scale:
                one = one * jnp.bfloat16(SCALE)
            stage[kind, 2 * p] = jnp.where(low, one, turned(two))
            stage[kind, 2 * p + 1] = jnp.where(low, turned(one), two)

    loads[0].wait()
    loads[1].wait()
    pack(0, 0, 1, False)

    pl.semaphore_wait(
        barrier, 17 - stays.astype(jnp.int32) + has_cross.astype(jnp.int32)
    )

    rows = pl.ds(pl.multiple_of(y * 32, 32), 32)

    def to_slab(kind, i, act):
        dx, dy = OFFSETS[i]
        xd = lax.rem(x + dx, 4)
        yd = lax.rem(y + dy, 4)
        src = stage.at[kind, yd * 4 + xd]
        if kind == 0:
            dst = win.at[pl.ds(HALO + 2 * pair, 2), rows, :]
            landed = kv_recv.at[pair]
        else:
            dst = own_qd.at[pl.ds(2 * pair, 2), rows, :]
            landed = qd_recv.at[pair]
        remote = pltpu.make_async_remote_copy(
            src_ref=src,
            dst_ref=dst,
            send_sem=send_sem.at[kind, i],
            recv_sem=landed,
            device_id=(z * 8 + xd * 2 + home, yd),
            device_id_type=MESH,
        )
        if dx == 0 and dy == 0:
            if act == "start":
                local = pltpu.make_async_copy(src, dst, landed)
                pl.when(stays)(local.start)
                pl.when(jnp.logical_not(stays))(remote.start)
            else:
                pl.when(jnp.logical_not(stays))(remote.wait_send)
        elif act == "start":
            remote.start()
        else:
            remote.wait_send()

    for i in range(16):
        to_slab(0, i, "start")

    loads[2].wait()
    loads[3].wait()
    pack(1, 2, 3, True)
    for i in range(16):
        to_slab(1, i, "start")

    far = jnp.where(c == 0, 0, HALO + OWN)

    @pl.when(jnp.logical_not(has_cross))
    def _():
        far_land[...] = jnp.zeros_like(far_land)
        cross_in[...] = jnp.zeros_like(cross_in)

    def byte_wait(ref, sem):
        pltpu.make_async_copy(ref, ref, sem).wait()

    def flip(w):
        wint[w] = win[w].T

    passed = []
    for k in (1, 2, 0, 3):
        here = win.at[HALO + 2 * k : HALO + 2 * k + 2]
        byte_wait(here, kv_recv.at[k])
        to_partner = pltpu.make_async_remote_copy(
            src_ref=here,
            dst_ref=win.at[pl.ds(jnp.where(c == 0, 2 * k - 2, HALO + OWN + 2 * k), 2)],
            send_sem=halo_send.at[0, k],
            recv_sem=halo_recv.at[0],
            device_id=(partner, y),
            device_id_type=MESH,
        )
        to_across = pltpu.make_async_remote_copy(
            src_ref=here,
            dst_ref=far_land.at[pl.ds(jnp.where(c == 0, 2 * k, 2 * k - 2), 2)],
            send_sem=halo_send.at[1, k],
            recv_sem=halo_recv.at[1],
            device_id=(across, y),
            device_id_type=MESH,
        )
        if k in (1, 2):
            crossing = has_cross
            to_partner.start()
            passed.append((None, to_partner))
        else:
            staying = (c == 1) if k == 0 else (c == 0)
            crossing = jnp.logical_and(has_cross, jnp.logical_not(staying))
            pl.when(staying)(to_partner.start)
            passed.append((staying, to_partner))
        pl.when(crossing)(to_across.start)
        passed.append((crossing, to_across))
    part_copy.wait()

    base = pos * OWN - HALO

    def turned_frame(i):
        return jnp.where(c == 0, i, OWN - 1 - i)

    @pl.loop(0, OWN)
    def _(i):
        f = turned_frame(i)
        at_frame = pos * OWN + f
        for w in range(WIN):
            target = base + jnp.where(c == 0, w, WIN - 1 - w)
            at = jnp.int32(ZERO)
            for s in range(SLOTS):
                at = jnp.where(part[s, at_frame] == target, i * KEYS + 1 + s, at)
            table[i, w] = jnp.where(i + HALO == w, i * KEYS, at)

    terms[ZERO] = jnp.zeros((TOK, 128), jnp.float32)
    for f in range(OWN):
        flip(HALO + f)
    for k in range(4):
        byte_wait(own_qd.at[2 * k : 2 * k + 2], qd_recv.at[k])

    near = jnp.where(c == 0, HALO + OWN, 0)
    byte_wait(win.at[pl.ds(near, HALO)], halo_recv.at[0])
    for w in range(HALO):
        flip(near + w)

    half = lax.broadcasted_iota(jnp.int32, (TOK, 128), 1) < HEAD_DIM

    def slots_of(i):
        f = turned_frame(i)
        at = [f + HALO]
        bias = [None]
        for s in range(SLOTS):
            listed = part[s, pos * OWN + f]
            close = jnp.minimum(jnp.maximum(listed - base, 0), WIN - 1)
            at.append(jnp.where(listed >= 0, close, f + HALO))
            bias.append(jnp.where(listed >= 0, jnp.float32(0.0), jnp.float32(-jnp.inf)))
        return f, at, bias

    def block_diagonal(f):
        mixed = own_qd[f]
        none = jnp.zeros_like(mixed)
        return jnp.concatenate([jnp.where(half, none, mixed), jnp.where(half, mixed, none)], axis=0)

    def products(n):
        u = n % 2
        f, at, bias = slots_of(ORDER[n])
        keyed = jnp.concatenate([win[at[s]] for s in range(KEYS)], axis=0)
        both = lax.dot_general(
            keyed, block_diagonal(f), (((1,), (1,)), ((), ())), preferred_element_type=jnp.float32
        )
        top = None
        for s in range(KEYS):
            here = both[s * TOK : (s + 1) * TOK]
            score = here[:, 128:]
            if bias[s] is not None:
                score = score + bias[s]
            sc[u, s, :, :128] = here[:, :128]
            sc[u, s, :, 128:] = score
            most = jnp.max(score.reshape(16, 8, 128), axis=0)
            top = most if top is None else jnp.maximum(top, most)
        peaks[u] = top

    def exponentials(n):
        u = n % 2
        peak = jnp.max(peaks[u], axis=0, keepdims=True)
        total = jnp.zeros((8, 128), jnp.float32)
        dsum = jnp.zeros((8, 128), jnp.float32)
        for s in range(KEYS):
            e = jnp.exp(sc[u, s, :, 128:] - peak)
            sc[u, s, :, 128:] = e
            total = total + jnp.sum(e.reshape(16, 8, 128), axis=0)
            dsum = dsum + jnp.sum((e * sc[u, s, :, :128]).reshape(16, 8, 128), axis=0)
        inv = 1.0 / jnp.sum(total, axis=0, keepdims=True)
        return inv, jnp.sum(dsum, axis=0, keepdims=True) * inv

    def gradients(n, inv, delta):
        u = n % 2
        for s in range(KEYS):
            w = sc[u, s, :, 128:] * inv
            rows_at = slice(s * TOK, (s + 1) * TOK)
            pd[u, rows_at, :128] = w.astype(jnp.bfloat16)
            pd[u, rows_at, 128:] = (w * (sc[u, s, :, :128] - delta)).astype(jnp.bfloat16)

    def key_terms(n):
        u = n % 2
        prod = jnp.dot(pd[u], block_diagonal(turned_frame(ORDER[n])), preferred_element_type=jnp.float32)
        for s in range(KEYS):
            terms[ORDER[n] * KEYS + s] = prod[s * TOK : (s + 1) * TOK]

    def query_terms(n):
        u = n % 2
        f, at, _ = slots_of(ORDER[n])
        turned_kv = jnp.concatenate([wint[at[s]] for s in range(KEYS)], axis=1)
        res = jnp.dot(turned_kv, pd[u], preferred_element_type=jnp.float32)
        outcome = jnp.concatenate([res[:HEAD_DIM, 128:] * SCALE, res[HEAD_DIM:, :128]], axis=0)
        outs[0, f] = outcome.T.astype(jnp.bfloat16)

    def gathered(w):
        total = None
        for i in range(max(0, w - 2 * HALO), min(OWN, w + 1)):
            term = terms[table[i, w]]
            total = term if total is None else total + term
        return total

    def pair_of(j):
        return jnp.where(c == 0, j, 3 - j)

    def give_back(kind, j, act):
        k = pair_of(j)
        xs = 2 * c + lax.div(k, 2)
        cs = lax.rem(k, 2)
        for dy in range(4):
            ys = lax.rem(y + (2, 1, 3, 0)[dy], 4)
            src = outs.at[kind, pl.ds(2 * k, 2), pl.ds(pl.multiple_of(ys * 32, 32), 32), :]
            dst = ostage.at[kind, head]
            remote = pltpu.make_async_remote_copy(
                src_ref=src,
                dst_ref=dst,
                send_sem=out_send.at[kind, j, dy],
                recv_sem=out_recv.at[kind],
                device_id=(z * 8 + xs * 2 + cs, ys),
                device_id_type=MESH,
            )
            if dy == 3:
                mine = jnp.logical_and(xs == x, cs == c)
                if act == "start":
                    local = pltpu.make_async_copy(src, dst, out_recv.at[kind])
                    pl.when(mine)(local.start)
                    pl.when(jnp.logical_not(mine))(remote.start)
                else:
                    pl.when(jnp.logical_not(mine))(remote.wait_send)
            elif act == "start":
                remote.start()
            else:
                remote.wait_send()

    cross_copies = [
        pltpu.make_async_remote_copy(
            src_ref=cross_out.at[2 * j : 2 * j + 2],
            dst_ref=cross_in.at[2 * j : 2 * j + 2],
            send_sem=cross_send.at[j],
            recv_sem=cross_recv.at[j],
            device_id=(across, y),
            device_id_type=MESH,
        )
        for j in range(3)
    ]

    products(0)

    @pl.when(has_cross)
    def _():
        byte_wait(far_land, halo_recv.at[1])

    for w in range(HALO):
        win[far + w] = far_land[w]
        wint[far + w] = far_land[w].T

    for n in range(OWN + 1):
        if n + 1 < OWN:
            products(n + 1)
        if n < OWN:
            inv, delta = exponentials(n)
        if n > 0:
            key_terms(n - 1)
        if n < OWN:
            gradients(n, inv, delta)
        if n > 0:
            query_terms(n - 1)
        if n in (3, 5, 7, 8):
            j = (3, 5, 7, 8).index(n)
            if j < 3:
                for w in (2 * j, 2 * j + 1):
                    cross_out[w] = gathered(w).astype(jnp.bfloat16)
                pl.when(has_cross)(cross_copies[j].start)
            give_back(0, j, "start")

    ret_copies = []
    for j in range(3):
        for q in (2 * j, 2 * j + 1):
            die_out[q] = gathered(HALO + OWN + q).astype(jnp.bfloat16)
        copy = pltpu.make_async_remote_copy(
            src_ref=die_out.at[2 * j : 2 * j + 2],
            dst_ref=die_in.at[2 * j : 2 * j + 2],
            send_sem=ret_send.at[j],
            recv_sem=ret_recv.at[j],
            device_id=(partner, y),
            device_id_type=MESH,
        )
        copy.start()
        ret_copies.append(copy)
    for i in range(OWN):
        acc[i] = gathered(HALO + i)
    for j in (3, 2, 1, 0):
        sums = [acc[i] for i in (2 * j, 2 * j + 1)]
        if j < 3:
            pl.when(has_cross)(cross_copies[2 - j].wait_recv)
        if j > 0:
            ret_copies[3 - j].wait_recv()
        for n, i in enumerate((2 * j, 2 * j + 1)):
            total = sums[n]
            if i < HALO:
                total = total + cross_in[HALO - 1 - i].astype(jnp.float32)
            if j > 0:
                total = total + die_in[OWN - 1 - i].astype(jnp.float32)
            outs[1, turned_frame(i)] = total.astype(jnp.bfloat16)
        give_back(1, j, "start")

    for i in range(16):
        to_slab(0, i, "wait")
        to_slab(1, i, "wait")
    for wanted, copy in passed:
        if wanted is None:
            copy.wait_send()
        else:
            pl.when(wanted)(copy.wait_send)
    for copy in cross_copies:
        pl.when(has_cross)(copy.wait_send)
    for copy in ret_copies:
        copy.wait_send()
    for j in range(4):
        give_back(0, j, "wait")
        give_back(1, j, "wait")
    for kind in range(2):
        byte_wait(ostage.at[kind], out_recv.at[kind])


def per_device(query, keyed, valued, grad_out, partners):
    depth = lax.axis_size("frames") // 8
    dma = pltpu.SemaphoreType.DMA
    staged = pl.pallas_call(
        functools.partial(kernel, depth),
        out_shape=pltpu.VMEM((2, HEADS, 2, 32, 128), jnp.bfloat16),
        in_specs=[pl.BlockSpec(memory_space=pltpu.HBM)] * 5,
        out_specs=pl.BlockSpec(memory_space=pltpu.VMEM),
        scratch_shapes=[
            pltpu.VMEM((4, 2, 32, 1024), jnp.bfloat16),
            pltpu.VMEM((2, HEADS, 2, 32, 128), jnp.bfloat16),
            pltpu.VMEM((WIN, TOK, 128), jnp.bfloat16),
            pltpu.VMEM((HALO, TOK, 128), jnp.bfloat16),
            pltpu.VMEM((WIN, 128, TOK), jnp.bfloat16),
            pltpu.VMEM((OWN, TOK, 128), jnp.bfloat16),
            pltpu.VMEM((2, KEYS, TOK, 256), jnp.float32),
            pltpu.VMEM((2, KEYS * TOK, 256), jnp.bfloat16),
            pltpu.VMEM((ZERO + 1, TOK, 128), jnp.float32),
            pltpu.VMEM((2, 8, 128), jnp.float32),
            pltpu.VMEM((OWN, TOK, 128), jnp.float32),
            pltpu.VMEM((HALO, TOK, 128), jnp.bfloat16),
            pltpu.VMEM((HALO, TOK, 128), jnp.bfloat16),
            pltpu.VMEM((HALO, TOK, 128), jnp.bfloat16),
            pltpu.VMEM((HALO, TOK, 128), jnp.bfloat16),
            pltpu.VMEM((2, OWN, TOK, 128), jnp.bfloat16),
            pltpu.SMEM(partners.shape[::-1], jnp.int32),
            pltpu.SMEM((OWN, WIN), jnp.int32),
            dma((4,)),
            dma(()),
            dma((2, 16)),
            dma((4,)),
            dma((4,)),
            dma((2, 4)),
            dma((2,)),
            dma((3,)),
            dma((3,)),
            dma((3,)),
            dma((3,)),
            dma((2, 4, 4)),
            dma((2,)),
        ],
        compiler_params=pltpu.CompilerParams(collective_id=0, has_side_effects=True, vmem_limit_bytes=60 * 2**20),
    )(query, keyed, valued, grad_out, partners.T)
    return unpacked(staged, query.shape)


def solution(mesh):
    spec = P("frames", "heads", None)
    return jax.shard_map(
        per_device,
        mesh=mesh,
        in_specs=(spec, spec, spec, spec, P()),
        out_specs=(spec,) * 4,
        check_vma=False,
    )
```
